256 devices in a mesh: seq: 32 (over y, z), tp: 8 (over x, core).
Axes of the slice: x: 4, y: 4, z: 8, core: 2. Of those that a mesh axis runs over, the one named last changes fastest.
Arguments:
- values_in: bfloat16 [16384, 8192], P('seq', 'tp'), may hold values from -6 to 6
- gates_in: bfloat16 [16384, 8192], P('seq', 'tp'), may hold values from -6 to 6
- keys_in: bfloat16 [16384, 1024], P('seq', 'tp'), may hold values from -6 to 6
- queries_in: bfloat16 [16384, 1024], P('seq', 'tp'), may hold values from -6 to 6
- log_decay: float32 [128, 16384], P('tp', 'seq'), may hold values from -2 to 0, as said below
- conv_values: float32 [4, 8192], P(None, 'tp'), may hold values from -3 to 3
- bias_values: float32 [8192], P('tp'), may hold values from -3 to 3
- conv_keys: float32 [4, 1024], P(None, 'tp'), may hold values from -3 to 3
- bias_keys: float32 [1024], P('tp'), may hold values from -3 to 3
- conv_queries: float32 [4, 1024], P(None, 'tp'), may hold values from -3 to 3
- bias_queries: float32 [1024], P('tp'), may hold values from -3 to 3
- skip_scale: float32 [128], P('tp'), may hold values from 0.5 to 1.5
- norm_gain: float32 [8192], P('tp'), may hold values from 0.1 to 1.9
- out_weight: bfloat16 [8192, 4096], P('tp'), may hold values from -0.09375 to 0.09375
Outputs:
- mixer_out: bfloat16 [16384, 4096], P('seq', 'tp')
The draws below stay inside these ranges and needn't reach their ends.
Inputs may be any that keep to these rules, and one draw needn't show every extreme that they name: `log_decay`: every entry is below zero.
All inputs are finite; a program needn't handle non-finite values.
Results may differ from the reference program's by a relative error of at most 0.015.
Values may be sent and summed in bfloat16 or wider, within the bound.
A program may use at most 64 MiB of HBM per device.

```python
import math
from functools import partial
import jax
import jax.numpy as jnp
from jax import lax

D = 4096
MIXER_HEADS = 128
P_SIZE = 64
N = 128
G = 8
KCONV = 4
TOK_DEV = 512
DI = 8192
SEQUENCE_TOKENS = 16384
BLOCK = 512
N_TP = 8


def draw_log_decay(key, part):
    random_subkeys = jax.random.split(jax.random.fold_in(key, 7), 7)
    slow_share = 0.5
    slow_heads = jax.random.uniform(random_subkeys[0], (MIXER_HEADS,)) < slow_share
    slow_rate = jnp.exp(jax.random.uniform(random_subkeys[1], (MIXER_HEADS,), minval=math.log(0.15), maxval=math.log(0.6))) / SEQUENCE_TOKENS
    fast_rate = jnp.exp(jax.random.uniform(random_subkeys[2], (MIXER_HEADS,), minval=math.log(1.0 / 50.0), maxval=math.log(1.0 / 20.0)))
    head_rate = jnp.where(slow_heads, slow_rate, fast_rate)
    shard_count = SEQUENCE_TOKENS // TOK_DEV
    shard_factor = jnp.exp(jax.random.uniform(random_subkeys[3], (MIXER_HEADS, shard_count), minval=math.log(0.5), maxval=math.log(2.0)))
    shard_factor = jnp.repeat(shard_factor, TOK_DEV, axis=1)
    token_factor = jnp.exp(jax.random.uniform(random_subkeys[4], (MIXER_HEADS, SEQUENCE_TOKENS), minval=math.log(0.7), maxval=math.log(1.4)))
    drawn_result = -head_rate[:, None] * shard_factor * token_factor
    spike_positions = jax.random.randint(random_subkeys[5], (2,), 0, SEQUENCE_TOKENS)
    spike_log_values = jnp.log(jax.random.uniform(random_subkeys[6], (2, MIXER_HEADS), minval=0.5, maxval=0.8))
    chosen_positions = jnp.arange(SEQUENCE_TOKENS, dtype=jnp.int32)
    earliest_match = (chosen_positions == spike_positions[0]).astype(jnp.float32)
    later_match = (chosen_positions == spike_positions[1]).astype(jnp.float32)
    spike_values = spike_log_values[0][:, None] * earliest_match[None, :] + spike_log_values[1][:, None] * later_match[None, :]
    return (drawn_result + spike_values).astype(jnp.float32)


def strengthened(array, stream_key, source, target, parts, factor):
    owner, partner = [(jnp.arange(array.shape[position]) // (array.shape[position] // parts)).reshape([-1 if axis == position else 1 for axis in range(array.ndim)]) for position in (source, target)]
    chosen = jax.random.permutation(stream_key, parts)[partner]
    strong = (owner == chosen) | (owner == (partner + parts // 2) % parts)
    return jnp.where(strong, factor * array, array)


def shard_levels(stream_key, shape, cuts, low, largest):
    loudness, own = 1.0, jax.random.fold_in(stream_key, 6)
    for dim, blocks in cuts:
        draws = jnp.exp(jax.random.uniform(jax.random.fold_in(own, dim), (blocks,), jnp.float32, low / len(cuts), largest / len(cuts)))
        loudness = loudness * jnp.repeat(draws, shape[dim] // blocks).reshape([-1 if axis == dim else 1 for axis in range(len(shape))])
    return loudness


def bell_draw(rng, shape, scale, most, shards=(), kind=jnp.bfloat16):
    drawn = scale * jax.random.normal(rng, shape, jnp.float32)
    if shards:
        drawn = drawn * shard_levels(rng, shape, shards, -0.22, 0.18)
    return jnp.clip(drawn, -most, most).astype(kind)


def bell_draw_with(own_key, shape, scale, most, cuts, heavy, held_as=jnp.bfloat16):
    array = scale * jax.random.normal(own_key, shape, jnp.float32)
    if cuts:
        array = array * shard_levels(own_key, shape, cuts, -0.22, 0.18)
    return jnp.clip(strengthened(array, jax.random.fold_in(own_key, 3), *heavy), -most, most).astype(held_as)


def setup_inputs(seed: int = 0) -> dict:
    seeds = jax.random.split(jax.random.key(seed), 15)
    return {
        "values_in": bell_draw(seeds[0], (SEQUENCE_TOKENS, DI), 1.0, 6.0, ((0, 32), (1, 8))),
        "gates_in": bell_draw(seeds[1], (SEQUENCE_TOKENS, DI), 1.0, 6.0, ((0, 32), (1, 8))),
        "keys_in": bell_draw(seeds[2], (SEQUENCE_TOKENS, G * N), 1.0, 6.0, ((0, 32), (1, 8))),
        "queries_in": bell_draw(seeds[3], (SEQUENCE_TOKENS, G * N), 1.0, 6.0, ((0, 32), (1, 8))),
        "log_decay": draw_log_decay(jax.random.fold_in(seeds[14], 71), 0),
        "conv_values": bell_draw(seeds[5], (KCONV, DI), KCONV ** -0.5, 3.0, ((1, 8),), jnp.float32),
        "bias_values": bell_draw(seeds[6], (DI,), 0.5, 3.0, ((0, 8),), jnp.float32),
        "conv_keys": bell_draw(seeds[7], (KCONV, G * N), KCONV ** -0.5, 3.0, ((1, 8),), jnp.float32),
        "bias_keys": bell_draw(seeds[8], (G * N,), 0.5, 3.0, ((0, 8),), jnp.float32),
        "conv_queries": bell_draw(seeds[9], (KCONV, G * N), KCONV ** -0.5, 3.0, ((1, 8),), jnp.float32),
        "bias_queries": bell_draw(seeds[10], (G * N,), 0.5, 3.0, ((0, 8),), jnp.float32),
        "skip_scale": jnp.clip(0.5 + 1.0 * jax.random.uniform(seeds[11], (MIXER_HEADS,), jnp.float32) ** shard_levels(seeds[11], (MIXER_HEADS,), ((0, 8),), -0.2, 0.2), 0.5, 1.5),
        "norm_gain": jnp.clip(1.0 + 0.18 * jax.random.normal(seeds[12], (DI,), jnp.float32), 0.1, 1.9),
        "out_weight": bell_draw_with(seeds[13], (DI, D), DI ** -0.5, 0.09375, ((0, 8),), (0, 1, 8, 2.0)),
    }


HIGH = lax.Precision.HIGHEST
norm_epsilon = 1e-05

def causal_filter(padded, kernel_weights, conv_bias, row_total):
    width = kernel_weights.shape[0]
    running = jnp.broadcast_to(conv_bias[None, :], (row_total, conv_bias.shape[0]))
    for offset in range(width):
        running = running + kernel_weights[offset][None, :] * padded[offset:offset + row_total].astype(jnp.float32)
    return jax.nn.silu(running).astype(jnp.bfloat16)

def filtered(raw_rows, kernel_weights, conv_bias):
    margin = kernel_weights.shape[0] - 1
    padded = jnp.concatenate([jnp.zeros((margin, raw_rows.shape[1]), raw_rows.dtype), raw_rows], axis=0)
    return causal_filter(padded, kernel_weights, conv_bias, raw_rows.shape[0])

def block_terms(carried, inputs, per_group):
    values, keys_block, queries, logs = inputs
    row_total = values.shape[0]
    groups = keys_block.shape[1]
    cumulative = jnp.cumsum(logs, axis=1)
    scores = jnp.einsum('tgn,sgn->gts', queries.astype(jnp.float32), keys_block.astype(jnp.float32), precision=HIGH)
    positions = lax.broadcasted_iota(jnp.int32, (row_total, row_total), 0)
    sources = lax.broadcasted_iota(jnp.int32, (row_total, row_total), 1)
    log_gaps = jnp.where((positions >= sources)[None], cumulative[:, :, None] - cumulative[:, None, :], -jnp.inf)
    mixing = (jnp.exp(log_gaps).reshape(groups, per_group, row_total, row_total) * scores[:, None]).astype(jnp.bfloat16)
    local_part = jnp.einsum('ghts,sghp->tghp', mixing.astype(jnp.float32), values.astype(jnp.float32), precision=HIGH)
    growth = jnp.exp(cumulative).T.reshape(row_total, groups, per_group, 1)
    from_state = jnp.einsum('tgn,ghnp->tghp', queries.astype(jnp.float32), carried, precision=HIGH) * growth
    remaining = jnp.exp(cumulative[:, -1:] - cumulative).T.reshape(row_total, groups, per_group, 1)
    weighted_keys = keys_block.astype(jnp.float32)[:, :, None, :] * remaining
    fresh_state = jnp.einsum('tghn,tghp->ghnp', weighted_keys, values.astype(jnp.float32), precision=HIGH)
    carried = jnp.exp(cumulative[:, -1]).reshape(groups, per_group, 1, 1) * carried + fresh_state
    return (carried, local_part + from_state)

def reference(values_in, gates_in, keys_in, queries_in, log_decay, conv_values, bias_values, conv_keys, bias_keys, conv_queries, bias_queries, skip_scale, norm_gain, out_weight):
    per_group = MIXER_HEADS // G
    block_count = SEQUENCE_TOKENS // BLOCK
    values = filtered(values_in, conv_values, bias_values)
    keys_all = filtered(keys_in, conv_keys, bias_keys)
    queries_all = filtered(queries_in, conv_queries, bias_queries)
    value_blocks = values.reshape(block_count, BLOCK, G, per_group, P_SIZE)
    key_blocks = keys_all.reshape(block_count, BLOCK, G, N)
    query_blocks = queries_all.reshape(block_count, BLOCK, G, N)
    log_blocks = log_decay.reshape(MIXER_HEADS, block_count, BLOCK).transpose(1, 0, 2)
    initial = jnp.zeros((G, per_group, N, P_SIZE), jnp.float32)
    last_state, outputs = lax.scan(partial(block_terms, per_group=per_group), initial, (value_blocks, key_blocks, query_blocks, log_blocks))
    mixed = outputs.reshape(SEQUENCE_TOKENS, G, per_group, P_SIZE)
    mixed = mixed + skip_scale.reshape(G, per_group)[None, :, :, None] * values.reshape(SEQUENCE_TOKENS, G, per_group, P_SIZE).astype(jnp.float32)
    gated_rows = mixed.reshape(SEQUENCE_TOKENS, G, per_group * P_SIZE) * jax.nn.silu(gates_in.reshape(SEQUENCE_TOKENS, G, per_group * P_SIZE).astype(jnp.float32))
    mean_square = lax.optimization_barrier(jnp.mean(gated_rows * gated_rows, axis=-1, keepdims=True))
    normed = (gated_rows * lax.rsqrt(mean_square + norm_epsilon) * norm_gain.reshape(G, per_group * P_SIZE)).astype(jnp.bfloat16).reshape(SEQUENCE_TOKENS, DI)
    column_width = DI // N_TP
    summed = jnp.zeros((SEQUENCE_TOKENS, D), jnp.float32)
    for member in range(N_TP):
        term_rows = jnp.dot(normed[:, member * column_width:(member + 1) * column_width], out_weight[member * column_width:(member + 1) * column_width], preferred_element_type=jnp.float32)
        term_rows = lax.optimization_barrier(term_rows.astype(jnp.bfloat16)).astype(jnp.float32)
        summed = summed + term_rows
    return summed.astype(jnp.bfloat16)
```

```python
import functools

import jax
import jax.numpy as jnp
from jax import lax
from jax.experimental import pallas as pl
from jax.experimental.pallas import tpu as pltpu
from jax.sharding import PartitionSpec as P

MESH = pl.DeviceIdType.MESH
F32 = jnp.float32
BF16 = jnp.bfloat16
EPS = 1e-05
CH = 128
PAD = 16
LANES = 128


def dot(a, b):
    return jnp.dot(a, b, preferred_element_type=F32)


def silu(v):
    h = 0.5 * v
    return h + h * jnp.tanh(h)


def parts_of(x):
    hi = x.astype(BF16).astype(F32)
    rest = x - hi
    mid = rest.astype(BF16).astype(F32)
    return hi, mid, rest - mid


def kernel(
    n_seq,
    v_hbm,
    g_hbm,
    k_hbm,
    q_hbm,
    log_ref,
    cv_ref,
    bv_ref,
    ck_ref,
    bk_ref,
    cq_ref,
    bq_ref,
    skip_ref,
    gain_ref,
    w_hbm,
    out_ref,
    xpad,
    gates,
    wbuf,
    spread,
    ct,
    cs,
    grow,
    rem,
    ap,
    vals,
    vw,
    keys_t,
    qs,
    fresh,
    s_loc,
    mixed,
    abuf,
    ra,
    fbuf,
    rf,
    sbuf,
    s_in,
    y,
    p_send,
    p_recv,
    own,
    h_send,
    h_recv,
    d_send,
    d_recv,
    c_send,
    c_recv,
    in_sem,
    w_sem,
    halo_s,
    halo_r,
    a_s,
    a_r,
    f_s,
    f_r,
    s_s,
    s_r,
    p_s,
    p_r,
    h_s,
    h_r,
    d_s,
    d_r,
    c_s,
    c_r,
):
    rows, width = v_hbm.shape
    heads = log_ref.shape[0]
    chunks = rows // CH
    slabs = width // LANES
    split = n_seq // slabs
    seg = 128 // split
    half = rows // 2
    quarter = half // 2
    tp_size = lax.axis_size("tp")
    me = lax.axis_index("seq")
    tp = lax.axis_index("tp")
    core = lax.rem(tp, 2)
    mate = tp + 1 - 2 * core
    ahead = lax.rem(tp + 2, tp_size)
    behind = lax.rem(tp + tp_size - 2, tp_size)
    far = lax.rem(tp + 4, tp_size)

    barrier = pltpu.get_barrier_semaphore()

    def greet(i, _):
        pl.semaphore_signal(
            barrier, inc=1, device_id={"seq": lax.rem(me + i, n_seq)}, device_id_type=MESH
        )
        return 0

    lax.fori_loop(1, n_seq, greet, 0)
    for other in (mate, ahead, behind):
        pl.semaphore_signal(barrier, inc=1, device_id={"tp": other}, device_id_type=MESH)

    loads = [
        pltpu.make_async_copy(v_hbm, xpad.at[pl.ds(PAD, rows), pl.ds(0, width)], in_sem.at[0]),
        pltpu.make_async_copy(
            k_hbm, xpad.at[pl.ds(PAD, rows), pl.ds(width, 128)], in_sem.at[1]
        ),
        pltpu.make_async_copy(
            q_hbm, xpad.at[pl.ds(PAD, rows), pl.ds(width + 128, 128)], in_sem.at[2]
        ),
        pltpu.make_async_copy(g_hbm, gates, in_sem.at[3]),
    ]
    for load in loads:
        load.start()
    cols = w_hbm.shape[1] // tp_size
    w_loads = []
    for j in range(8):
        chip = (far, ahead, behind, tp)[j // 2]
        owner = chip - core + (1 - core if j % 2 == 0 else core)
        w_loads.append(
            pltpu.make_async_copy(
                w_hbm.at[:, pl.ds(pl.multiple_of(owner * cols, cols), cols)],
                wbuf.at[j],
                w_sem.at[j],
            )
        )
    for load in w_loads:
        load.start()

    lane_head = lax.broadcasted_iota(jnp.int32, (2 * heads, width), 1) // (width // heads)
    row_head = lax.broadcasted_iota(jnp.int32, (2 * heads, width), 0)
    row_head = jnp.where(row_head >= heads, row_head - heads, row_head)
    spread[...] = jnp.where(lane_head == row_head, 1.0, 0.0).astype(BF16)

    def expand(x):
        hi = x.astype(BF16).astype(F32)
        return jnp.concatenate([hi, x - hi], axis=1).astype(BF16)

    low_a = lax.broadcasted_iota(jnp.int32, (CH, CH), 0)
    low_b = lax.broadcasted_iota(jnp.int32, (CH, CH), 1)
    lower = jnp.where(low_b <= low_a, 1.0, 0.0)
    lower3 = jnp.concatenate([lower] * 3, axis=1).astype(BF16)
    upper = jnp.where(low_a <= low_b, 1.0, 0.0)
    upper3 = jnp.concatenate([upper] * 3, axis=0).astype(BF16)

    def decay(c, _):
        at = pl.ds(pl.multiple_of(c * CH, CH), CH)
        logs = jnp.concatenate(parts_of(log_ref[:, at]), axis=1).astype(BF16)
        col = lax.dot_general(lower3, logs, (((1,), (1,)), ((), ())), preferred_element_type=F32)
        ct[c] = col
        cs[c] = dot(logs, upper3)
        g2 = expand(jnp.exp(col))
        r2 = expand(jnp.exp(jnp.minimum(col[CH - 1 : CH, :] - col, 0.0)))
        for j in range(width // 256):
            sl = slice(j * 256, (j + 1) * 256)
            grow[at, sl] = dot(g2, spread[:, sl])
            rem[at, sl] = dot(r2, spread[:, sl])
        return 0

    lax.fori_loop(0, chunks, decay, 0)
    before = jnp.ones((1, width), F32)
    for c in range(chunks):
        ap[c] = jnp.broadcast_to(before, (8, width))
        before = before * grow[c * CH + CH - 1 : c * CH + CH, :]
    for q in range(slabs):
        abuf[q] = jnp.broadcast_to(before[:, q * LANES : (q + 1) * LANES], (8, LANES))
    skip8 = jnp.broadcast_to(skip_ref[...], (8, heads))

    pl.semaphore_wait(barrier, n_seq - 1 + 3)

    after = {"seq": lax.rem(me + 1, n_seq)}
    halos = []
    for i, (src, lo, wid) in enumerate(
        ((v_hbm, 0, width), (k_hbm, width, 128), (q_hbm, width + 128, 128))
    ):
        halos.append(
            pltpu.make_async_remote_copy(
                src_ref=src.at[pl.ds(rows - PAD, PAD), :],
                dst_ref=xpad.at[pl.ds(0, PAD), pl.ds(lo, wid)],
                send_sem=halo_s.at[i],
                recv_sem=halo_r.at[i],
                device_id=after,
                device_id_type=MESH,
            )
        )
    for halo in halos:
        halo.start()

    def a_copy(peer, slot):
        return pltpu.make_async_remote_copy(
            src_ref=abuf.at[peer // split],
            dst_ref=ra.at[slot],
            send_sem=a_s.at[peer],
            recv_sem=a_r.at[slot],
            device_id={"seq": peer},
            device_id_type=MESH,
        )

    def f_copy(peer, slot):
        return pltpu.make_async_remote_copy(
            src_ref=fbuf.at[peer],
            dst_ref=rf.at[slot],
            send_sem=f_s.at[peer],
            recv_sem=f_r.at[slot],
            device_id={"seq": peer},
            device_id_type=MESH,
        )

    def s_copy(peer, slot):
        return pltpu.make_async_remote_copy(
            src_ref=sbuf.at[peer],
            dst_ref=s_in.at[slot],
            send_sem=s_s.at[peer],
            recv_sem=s_r.at[slot],
            device_id={"seq": peer},
            device_id_type=MESH,
        )

    def send_a(i, _):
        a_copy(lax.rem(me + i, n_seq), me).start()
        return 0

    lax.fori_loop(1, n_seq, send_a, 0)
    ra[me] = abuf[me // split]

    def conv(c):
        at = pl.ds(pl.multiple_of(c * CH, CH), CH)
        window = pl.ds(pl.multiple_of(c * CH, CH), CH + PAD)

        def taps(lo, w_ref, b_ref, off):
            x = xpad[window, lo : lo + LANES].astype(F32)
            sl = slice(off, off + LANES)
            acc = b_ref[:, sl] + w_ref[3:4, sl] * x[PAD:]
            for back in range(1, 4):
                acc = acc + w_ref[3 - back : 4 - back, sl] * pltpu.roll(x, back, axis=0)[PAD:]
            return silu(acc).astype(BF16)

        keys = taps(width, ck_ref, bk_ref, 0)
        kt = keys.astype(F32).T.astype(BF16)
        keys_t[c] = kt
        qs[at, :] = taps(width + 128, cq_ref, bq_ref, 0)
        for j in range(slabs):
            sl = slice(j * LANES, (j + 1) * LANES)
            v = taps(j * LANES, cv_ref, bv_ref, j * LANES)
            vals[at, sl] = v
            vw[:, sl] = (v.astype(F32) * rem[at, sl]).astype(BF16)
        for j in range(width // 256):
            sl = slice(j * 256, (j + 1) * 256)
            fresh[c, :, sl] = dot(kt, vw[:, sl])

    for load in loads[:3]:
        load.wait()

    def conv_step(i, _):
        conv(chunks - i)
        return 0

    lax.fori_loop(1, chunks, conv_step, 0)
    for halo in halos:
        halo.wait_recv()

    @pl.when(me == 0)
    def _():
        xpad[0:PAD, :] = jnp.zeros((PAD, xpad.shape[1]), BF16)

    conv(0)

    for q in range(slabs):
        sl = slice(q * LANES, (q + 1) * LANES)
        s = fresh[0, :, sl]
        s_loc[0, :, sl] = jnp.zeros((128, LANES), BF16)
        for c in range(1, chunks):
            s_loc[c, :, sl] = s.astype(BF16)
            s = grow[c * CH + CH - 1 : c * CH + CH, sl] * s + fresh[c, :, sl]
        f = s.astype(BF16)
        for r in range(split):
            fbuf[q * split + r] = f[r * seg : (r + 1) * seg]

    def send_f(i, _):
        f_copy(lax.rem(me + i, n_seq), me).start()
        return 0

    lax.fori_loop(1, n_seq, send_f, 0)
    rf[me] = fbuf[me]

    skip_row = dot(expand(skip8), spread[...])
    lane = lax.broadcasted_iota(jnp.int32, (1, LANES), 1)
    first = jnp.where(lane < LANES // 2, 1.0, 0.0).astype(BF16)
    second = jnp.where(lane < LANES // 2, 0.0, 1.0).astype(BF16)

    def local(c, _):
        at = pl.ds(pl.multiple_of(c * CH, CH), CH)
        qc = qs[at, :]
        scores = jnp.where(low_b <= low_a, dot(qc, keys_t[c]), 0.0)
        for q in range(slabs):
            sl = slice(q * LANES, (q + 1) * LANES)
            mixes = []
            for h in (2 * q, 2 * q + 1):
                gap = ct[c, :, h : h + 1] - cs[c, h : h + 1, :]
                mixes.append((jnp.exp(jnp.minimum(gap, 0.0)) * scores).astype(BF16))
            v = vals[at, sl]
            rhs = jnp.concatenate([v * first, v * second], axis=0)
            o = dot(jnp.concatenate(mixes, axis=1), rhs)
            g = grow[at, sl]
            o = o + g * dot(qc, s_loc[c, :, sl])
            mixed[at, sl] = o + skip_row[0:1, sl] * v.astype(F32)
            grow[at, sl] = g * ap[c, 0:1, sl]
        return 0

    lax.fori_loop(0, chunks, local, 0)

    def scan(b, s):
        @pl.when(b != me)
        def _():
            a_copy(b, b).wait_recv()
            f_copy(b, b).wait_recv()

        out = s.astype(BF16).reshape(seg, LANES)
        sbuf[b] = out

        @pl.when(b != me)
        def _():
            s_copy(b, me).start()

        @pl.when(b == me)
        def _():
            s_in[b] = out

        return ra[b][None] * s + rf[b].astype(F32).reshape(seg // 8, 8, LANES)

    lax.fori_loop(0, n_seq, scan, jnp.zeros((seg // 8, 8, LANES), F32))

    loads[3].wait()

    def gate(i, _):
        at = pl.ds(pl.multiple_of(i * 16, 16), 16)
        s = silu(gates[at, :].astype(F32))
        mixed[at, :] = mixed[at, :] * s
        grow[at, :] = grow[at, :] * s
        return 0

    lax.fori_loop(0, rows // 16, gate, 0)
    for load in w_loads:
        load.wait()

    def await_s(i, _):
        b = lax.rem(me + i, n_seq)
        s_copy(b, b).wait_recv()
        return 0

    lax.fori_loop(1, n_seq, await_s, 0)

    def finish_rows(m):
        top = m * half
        at = slice(top, top + half)
        qm = qs[at, :]
        total = jnp.zeros((half, LANES), F32)
        for j in range(width // 256):
            pair = [
                s_in[(2 * j + i) * split : (2 * j + i + 1) * split].reshape(128, LANES)
                for i in range(2)
            ]
            t = dot(qm, jnp.concatenate(pair, axis=1))
            sl = slice(j * 256, (j + 1) * 256)
            x = mixed[at, sl] + grow[at, sl] * t
            mixed[at, sl] = x
            total = total + x[:, :LANES] * x[:, :LANES] + x[:, LANES:] * x[:, LANES:]
        scale = lax.rsqrt(jnp.sum(total, axis=1, keepdims=True) * (1.0 / width) + EPS)
        for j in range(slabs):
            sl = slice(j * LANES, (j + 1) * LANES)
            y[at, sl] = (mixed[at, sl] * scale * gain_ref[:, sl]).astype(BF16)

    def p_copy(m, k):
        return pltpu.make_async_remote_copy(
            src_ref=p_send.at[m, k],
            dst_ref=p_recv.at[m, k],
            send_sem=p_s.at[m, k],
            recv_sem=p_r.at[m, k],
            device_id={"tp": mate},
            device_id_type=MESH,
        )

    def x_copy(send, recv, ss, rs, m, way):
        return pltpu.make_async_remote_copy(
            src_ref=send.at[m, way],
            dst_ref=recv.at[m, way],
            send_sem=ss.at[m, way],
            recv_sem=rs.at[m, way],
            device_id={"tp": ahead if way == 0 else behind},
            device_id_type=MESH,
        )

    def h_copy(m, way):
        return x_copy(h_send, h_recv, h_s, h_r, m, way)

    def d_copy(m, way):
        return x_copy(d_send, d_recv, d_s, d_r, m, way)

    def c_copy(m, way):
        return x_copy(c_send, c_recv, c_s, c_r, m, way)

    def multiply(m, k):
        at = slice(m * half, (m + 1) * half)
        p_send[m, k] = dot(y[at, :], wbuf[2 * k]).astype(BF16)
        p_copy(m, k).start()
        own[m, k] = dot(y[at, :], wbuf[2 * k + 1])

    def chip_sum(m, k, lo):
        at = slice(lo, lo + quarter)
        return own[m, k, at, :] + p_recv[m, k, at, :].astype(F32)

    def send_far(m):
        p_copy(m, 0).wait_recv()
        h_send[m, 0] = chip_sum(m, 0, 0).astype(BF16)
        h_copy(m, 0).start()
        h_send[m, 1] = chip_sum(m, 0, quarter).astype(BF16)
        h_copy(m, 1).start()

    def send_near(m, way):
        p_copy(m, 1 + way).wait_recv()
        d_send[m, way] = chip_sum(m, 1 + way, quarter if way == 0 else 0).astype(BF16)
        d_copy(m, way).start()

    def send_joined(m, way):
        h_copy(m, way).wait_recv()
        part = chip_sum(m, 1 + way, 0 if way == 0 else quarter)
        c_send[m, way] = (part + h_recv[m, way].astype(F32)).astype(BF16)
        c_copy(m, way).start()

    def close(m):
        p_copy(m, 3).wait_recv()
        for way in range(2):
            d_copy(m, 1 - way).wait_recv()
            c_copy(m, way).wait_recv()
            lo = way * quarter
            total = chip_sum(m, 3, lo)
            total = total + d_recv[m, 1 - way].astype(F32) + c_recv[m, way].astype(F32)
            out_ref[m * half + lo : m * half + lo + quarter, :] = total.astype(BF16)

    finish_rows(0)
    multiply(0, 0)
    multiply(0, 1)
    send_far(0)
    multiply(0, 2)
    send_near(0, 0)
    finish_rows(1)
    send_near(0, 1)
    multiply(1, 0)
    send_joined(0, 0)
    send_joined(0, 1)
    multiply(1, 1)
    send_far(1)
    multiply(1, 2)
    send_near(1, 0)
    multiply(0, 3)
    send_near(1, 1)
    multiply(1, 3)
    send_joined(1, 0)
    send_joined(1, 1)
    close(0)
    close(1)

    for halo in halos:
        halo.wait_send()

    def drain(i, _):
        b = lax.rem(me + i, n_seq)
        a_copy(b, me).wait_send()
        f_copy(b, me).wait_send()
        s_copy(b, me).wait_send()
        return 0

    lax.fori_loop(1, n_seq, drain, 0)
    for m in range(2):
        for k in range(4):
            p_copy(m, k).wait_send()
        for way in range(2):
            h_copy(m, way).wait_send()
            d_copy(m, way).wait_send()
            c_copy(m, way).wait_send()


def shards(
    n_seq,
    values_in,
    gates_in,
    keys_in,
    queries_in,
    log_decay,
    conv_values,
    bias_values,
    conv_keys,
    bias_keys,
    conv_queries,
    bias_queries,
    skip_scale,
    norm_gain,
    out_weight,
):
    rows, width = values_in.shape
    heads = log_decay.shape[0]
    chunks = rows // CH
    slabs = width // LANES
    seg = 128 * slabs // n_seq
    half, quarter = rows // 2, rows // 4
    depth, full = out_weight.shape
    cols = full // 8
    vmem = pl.BlockSpec(memory_space=pltpu.VMEM)
    hbm = pl.BlockSpec(memory_space=pl.ANY)
    dma = pltpu.SemaphoreType.DMA
    return pl.pallas_call(
        functools.partial(kernel, n_seq),
        out_shape=jax.ShapeDtypeStruct((rows, cols), BF16),
        in_specs=[hbm] * 4 + [vmem] * 9 + [hbm],
        out_specs=vmem,
        scratch_shapes=[
            pltpu.VMEM((rows + PAD, width + 256), BF16),
            pltpu.VMEM((rows, width), BF16),
            pltpu.VMEM((8, depth, cols), BF16),
            pltpu.VMEM((2 * heads, width), BF16),
            pltpu.VMEM((chunks, CH, heads), F32),
            pltpu.VMEM((chunks, heads, CH), F32),
            pltpu.VMEM((rows, width), F32),
            pltpu.VMEM((rows, width), F32),
            pltpu.VMEM((chunks, 8, width), F32),
            pltpu.VMEM((rows, width), BF16),
            pltpu.VMEM((CH, width), BF16),
            pltpu.VMEM((chunks, 128, CH), BF16),
            pltpu.VMEM((rows, 128), BF16),
            pltpu.VMEM((chunks, 128, width), F32),
            pltpu.VMEM((chunks, 128, width), BF16),
            pltpu.VMEM((rows, width), F32),
            pltpu.VMEM((slabs, 8, LANES), F32),
            pltpu.VMEM((n_seq, 8, LANES), F32),
            pltpu.VMEM((n_seq, seg, LANES), BF16),
            pltpu.VMEM((n_seq, seg, LANES), BF16),
            pltpu.VMEM((n_seq, seg, LANES), BF16),
            pltpu.VMEM((n_seq, seg, LANES), BF16),
            pltpu.VMEM((rows, width), BF16),
            pltpu.VMEM((2, 4, half, cols), BF16),
            pltpu.VMEM((2, 4, half, cols), BF16),
            pltpu.VMEM((2, 4, half, cols), F32),
        ]
        + [pltpu.VMEM((2, 2, quarter, cols), BF16)] * 6
        + [dma((4,)), dma((8,)), dma((3,)), dma((3,))]
        + [dma((n_seq,))] * 6
        + [dma((2, 4))] * 2
        + [dma((2, 2))] * 6,
        compiler_params=pltpu.CompilerParams(collective_id=0, has_side_effects=True),
        name="mixer",
    )(
        values_in,
        gates_in,
        keys_in,
        queries_in,
        log_decay,
        conv_values,
        bias_values[None],
        conv_keys,
        bias_keys[None],
        conv_queries,
        bias_queries[None],
        skip_scale[None],
        norm_gain[None],
        out_weight,
    )


def solution(mesh):
    placed = (
        P("seq", "tp"),
        P("seq", "tp"),
        P("seq", "tp"),
        P("seq", "tp"),
        P("tp", "seq"),
        P(None, "tp"),
        P("tp"),
        P(None, "tp"),
        P("tp"),
        P(None, "tp"),
        P("tp"),
        P("tp"),
        P("tp"),
        P("tp", None),
    )
    return jax.shard_map(
        functools.partial(shards, mesh.shape["seq"]),
        mesh=mesh,
        in_specs=placed,
        out_specs=P("seq", "tp"),
        check_vma=False,
    )
```

```python
import functools

import jax
import jax.numpy as jnp
from jax import lax
from jax.experimental import pallas as pl
from jax.experimental.pallas import tpu as pltpu
from jax.sharding import PartitionSpec as P

MESH = pl.DeviceIdType.MESH
F32 = jnp.float32
BF16 = jnp.bfloat16
EPS = 1e-05
CH = 128
PAD = 16
LANES = 128
ROW = 8


def dot(a, b):
    return jnp.dot(a, b, preferred_element_type=F32)


def silu(v):
    h = 0.5 * v
    return h + h * jnp.tanh(h)


def parts_of(x):
    hi = x.astype(BF16).astype(F32)
    rest = x - hi
    mid = rest.astype(BF16).astype(F32)
    return hi, mid, rest - mid


def kernel(
    n_seq,
    v_hbm,
    g_hbm,
    k_hbm,
    q_hbm,
    log_hbm,
    cv_hbm,
    bv_hbm,
    ck_hbm,
    bk_hbm,
    cq_hbm,
    bq_hbm,
    skip_hbm,
    gain_hbm,
    w_hbm,
    out_ref,
    log_ref,
    cv_ref,
    bv_ref,
    ck_ref,
    bk_ref,
    cq_ref,
    bq_ref,
    skip_ref,
    gain_ref,
    xpad,
    edge,
    gates,
    w_own,
    w_mate,
    spread,
    shift,
    shift_top,
    ct,
    cs,
    grow,
    rem,
    ap,
    vals,
    vw,
    keys0,
    keys_t,
    qs,
    fresh,
    rest,
    s_loc,
    mixed,
    abuf,
    ra,
    fbuf,
    rf,
    sbuf,
    s_in,
    y,
    y_mate,
    first,
    own,
    join,
    h_send,
    h_recv,
    d_send,
    d_recv,
    c_send,
    c_recv,
    small_sem,
    in_sem,
    w_sem,
    wx_s,
    wx_r,
    halo_s,
    halo_r,
    a_s,
    a_r,
    f_s,
    f_r,
    s_s,
    s_r,
    y_s,
    y_r,
    h_s,
    h_r,
    d_s,
    d_r,
    c_s,
    c_r,
):
    rows, width = v_hbm.shape
    heads = log_ref.shape[0]
    hops = sorted(
        ((dy, dz) for dy in range(n_seq // ROW) for dz in range(ROW) if dy or dz),
        key=lambda o: -min(o[0], n_seq // ROW - o[0]) - min(o[1], ROW - o[1]),
    )
    chunks = rows // CH
    slabs = width // LANES
    split = n_seq // slabs
    seg = 128 // split
    half = rows // 2
    quarter = half // 2
    tp_size = lax.axis_size("tp")
    me = lax.axis_index("seq")
    tp = lax.axis_index("tp")
    core = lax.rem(tp, 2)
    mate = tp + 1 - 2 * core
    ahead = lax.rem(tp + 2, tp_size)
    behind = lax.rem(tp + tp_size - 2, tp_size)
    far = lax.rem(tp + 4, tp_size)

    barrier = pltpu.get_barrier_semaphore()

    def greet(i, _):
        pl.semaphore_signal(
            barrier, inc=1, device_id={"seq": lax.rem(me + i, n_seq)}, device_id_type=MESH
        )
        return 0

    lax.fori_loop(1, n_seq, greet, 0)
    for other in (mate, ahead, behind):
        pl.semaphore_signal(barrier, inc=1, device_id={"tp": other}, device_id_type=MESH)

    smalls = [
        pltpu.make_async_copy(src, dst, small_sem.at[i])
        for i, (src, dst) in enumerate(
            (
                (log_hbm, log_ref),
                (cv_hbm, cv_ref),
                (bv_hbm, bv_ref),
                (ck_hbm, ck_ref),
                (bk_hbm, bk_ref),
                (cq_hbm, cq_ref),
                (bq_hbm, bq_ref),
                (skip_hbm, skip_ref),
                (gain_hbm, gain_ref),
            )
        )
    ]
    loads = [
        pltpu.make_async_copy(v_hbm, xpad.at[pl.ds(PAD, rows), pl.ds(0, width)], in_sem.at[0]),
        pltpu.make_async_copy(
            k_hbm, xpad.at[pl.ds(PAD, rows), pl.ds(width, 128)], in_sem.at[1]
        ),
        pltpu.make_async_copy(
            q_hbm, xpad.at[pl.ds(PAD, rows), pl.ds(width + 128, 128)], in_sem.at[2]
        ),
    ]
    gate_load = pltpu.make_async_copy(g_hbm, gates, in_sem.at[3])
    for load in smalls + loads:
        load.start()
    cols = w_hbm.shape[1] // tp_size

    def w_part(k, side):
        chip = (far, ahead, behind, tp)[k] - core
        return w_hbm.at[:, pl.ds(pl.multiple_of((chip + side) * cols, cols), cols)]

    w_loads = [
        pltpu.make_async_copy(w_part(k, core), w_own.at[k], w_sem.at[k]) for k in range(4)
    ]

    def w_copy(k):
        return pltpu.make_async_remote_copy(
            src_ref=w_part(k, 1 - core),
            dst_ref=w_mate.at[k],
            send_sem=wx_s.at[k],
            recv_sem=wx_r.at[k],
            device_id={"tp": mate},
            device_id_type=MESH,
        )

    xpad[0:PAD, :] = jnp.zeros((PAD, xpad.shape[1]), BF16)
    for ref, span in ((shift, CH), (shift_top, PAD)):
        out_row = lax.broadcasted_iota(jnp.int32, ref.shape, 0)
        in_row = lax.broadcasted_iota(jnp.int32, ref.shape, 1)
        hit = out_row == -1
        for back in range(1, 4):
            base = (back - 1) * span
            here = (out_row >= base) & (out_row < base + span)
            hit = hit | (here & (in_row == out_row - base + PAD - back))
        ref[...] = jnp.where(hit, 1.0, 0.0).astype(BF16)

    lane_head = lax.broadcasted_iota(jnp.int32, (2 * heads, width), 1) // (width // heads)
    row_head = lax.broadcasted_iota(jnp.int32, (2 * heads, width), 0)
    row_head = jnp.where(row_head >= heads, row_head - heads, row_head)
    spread[...] = jnp.where(lane_head == row_head, 1.0, 0.0).astype(BF16)

    def expand(x):
        hi = x.astype(BF16).astype(F32)
        return jnp.concatenate([hi, x - hi], axis=1).astype(BF16)

    low_a = lax.broadcasted_iota(jnp.int32, (CH, CH), 0)
    low_b = lax.broadcasted_iota(jnp.int32, (CH, CH), 1)
    lower = jnp.where(low_b <= low_a, 1.0, 0.0)
    lower3 = jnp.concatenate([lower] * 3, axis=1).astype(BF16)
    upper = jnp.where(low_a <= low_b, 1.0, 0.0)
    upper3 = jnp.concatenate([upper] * 3, axis=0).astype(BF16)

    def decay(c, _):
        at = pl.ds(pl.multiple_of(c * CH, CH), CH)
        logs = jnp.concatenate(parts_of(log_ref[:, at]), axis=1).astype(BF16)
        col = lax.dot_general(lower3, logs, (((1,), (1,)), ((), ())), preferred_element_type=F32)
        ct[c] = col
        cs[c] = dot(logs, upper3)
        g2 = expand(jnp.exp(col))
        r2 = expand(jnp.exp(jnp.minimum(col[CH - 1 : CH, :] - col, 0.0)))
        for j in range(width // 256):
            sl = slice(j * 256, (j + 1) * 256)
            grow[at, sl] = dot(g2, spread[:, sl])
            rem[at, sl] = dot(r2, spread[:, sl])
        return 0

    smalls[0].wait()
    lax.fori_loop(0, chunks, decay, 0)
    before = jnp.ones((1, width), F32)
    for c in range(chunks):
        ap[c] = jnp.broadcast_to(before, (8, width))
        before = before * grow[c * CH + CH - 1 : c * CH + CH, :]
    for q in range(slabs):
        abuf[q] = jnp.broadcast_to(before[:, q * LANES : (q + 1) * LANES], (8, LANES))
    after = {"seq": lax.rem(me + 1, n_seq)}
    halos = []
    for i, (src, lo, wid) in enumerate(
        ((v_hbm, 0, width), (k_hbm, width, 128), (q_hbm, width + 128, 128))
    ):
        halos.append(
            pltpu.make_async_remote_copy(
                src_ref=src.at[pl.ds(rows - PAD, PAD), :],
                dst_ref=edge.at[:, pl.ds(lo, wid)],
                send_sem=halo_s.at[i],
                recv_sem=halo_r.at[i],
                device_id=after,
                device_id_type=MESH,
            )
        )

    def a_copy(peer, slot):
        return pltpu.make_async_remote_copy(
            src_ref=abuf.at[peer // split],
            dst_ref=ra.at[slot],
            send_sem=a_s.at[peer],
            recv_sem=a_r.at[slot],
            device_id={"seq": peer},
            device_id_type=MESH,
        )

    def f_copy(peer, slot):
        return pltpu.make_async_remote_copy(
            src_ref=fbuf.at[peer],
            dst_ref=rf.at[slot],
            send_sem=f_s.at[peer],
            recv_sem=f_r.at[slot],
            device_id={"seq": peer},
            device_id_type=MESH,
        )

    def s_copy(peer, slot):
        return pltpu.make_async_remote_copy(
            src_ref=sbuf.at[peer],
            dst_ref=s_in.at[slot],
            send_sem=s_s.at[peer],
            recv_sem=s_r.at[slot],
            device_id={"seq": peer},
            device_id_type=MESH,
        )

    def send_a(i, _):
        a_copy(lax.rem(me + i, n_seq), me).start()
        return 0

    def taps(x, shifted, span, w_ref, b_ref, sl):
        acc = b_ref[:, sl] + w_ref[3:4, sl] * x.astype(F32)
        for back in range(1, 4):
            acc = acc + w_ref[3 - back : 4 - back, sl] * shifted[(back - 1) * span : back * span]
        return silu(acc).astype(BF16)

    def conv(c, top):
        at = pl.ds(pl.multiple_of(c * CH, CH), CH)
        window = pl.ds(pl.multiple_of(c * CH, CH), CH + PAD)
        kq = slice(width, width + 256)
        x = xpad[window, kq]
        moved = dot(shift[...], x)
        one = slice(0, 128)
        keys = taps(x[PAD:, :128], moved[:, :128], CH, ck_ref, bk_ref, one)
        kt = keys.astype(F32).T.astype(BF16)
        keys_t[c] = kt
        if top:
            keys0[...] = keys
        qs[at, :] = taps(x[PAD:, 128:], moved[:, 128:], CH, cq_ref, bq_ref, one)
        for j in range(width // 256):
            sl = slice(j * 256, (j + 1) * 256)
            x = xpad[window, sl]
            v = taps(x[PAD:], dot(shift[...], x), CH, cv_ref, bv_ref, sl)
            vals[at, sl] = v
            weighted = (v.astype(F32) * rem[at, sl]).astype(BF16)
            if top:
                vw[:, sl] = weighted
                vw[0:PAD, sl] = jnp.zeros((PAD, 256), BF16)
                weighted = vw[:, sl]
            fresh[c, :, sl] = dot(kt, weighted)

    for load in smalls[1:] + loads:
        load.wait()
    gate_load.start()
    for load in w_loads:
        load.start()

    def conv_step(i, _):
        conv(chunks - i, False)
        return 0

    lax.fori_loop(1, 3, conv_step, 0)

    pl.semaphore_wait(barrier, n_seq - 1 + 3)
    for halo in halos:
        halo.start()
    lax.fori_loop(1, n_seq, send_a, 0)
    ra[me] = abuf[me // split]
    for k in range(4):
        w_copy(k).start()

    lax.fori_loop(3, chunks, conv_step, 0)
    conv(0, True)
    for q in range(slabs):
        sl = slice(q * LANES, (q + 1) * LANES)
        s = fresh[0, :, sl]
        for c in range(1, chunks):
            s = grow[c * CH + CH - 1 : c * CH + CH, sl] * s + fresh[c, :, sl]
        rest[:, sl] = s

    later = jnp.ones((1, width), F32)
    for c in range(1, chunks):
        later = later * grow[c * CH + CH - 1 : c * CH + CH, :]
    is_first = me == 0
    for halo in halos:
        halo.wait_recv()
    head = slice(0, PAD)

    def top_rows(sl):
        above = jnp.where(is_first, 0.0, edge[:, sl].astype(F32)).astype(BF16)
        here = xpad[PAD : 2 * PAD, sl]
        return here, dot(shift_top[...], jnp.concatenate([above, here], axis=0))

    x, moved = top_rows(slice(width, width + 256))
    keys0[head, :] = taps(x[:, :128], moved[:, :128], PAD, ck_ref, bk_ref, slice(0, 128))
    qs[head, :] = taps(x[:, 128:], moved[:, 128:], PAD, cq_ref, bq_ref, slice(0, 128))
    kt = keys0[...].astype(F32).T.astype(BF16)
    keys_t[0] = kt
    for j in range(width // 256):
        sl = slice(j * 256, (j + 1) * 256)
        x, moved = top_rows(sl)
        v = taps(x, moved, PAD, cv_ref, bv_ref, sl)
        vals[head, sl] = v
        weighted = (v.astype(F32) * rem[head, sl]).astype(BF16)
        more = dot(kt[:, :PAD], weighted)
        fresh[0, :, sl] = fresh[0, :, sl] + more
        f = (rest[:, sl] + later[:, sl] * more).astype(BF16)
        for i in range(2):
            for r in range(split):
                fbuf[(2 * j + i) * split + r] = f[
                    r * seg : (r + 1) * seg, i * LANES : (i + 1) * LANES
                ]

    def far_first(copy):
        for dy, dz in hops:
            at = lax.rem(me // ROW + dy, n_seq // ROW) * ROW + lax.rem(lax.rem(me, ROW) + dz, ROW)
            copy(at, me).start()

    far_first(f_copy)
    rf[me] = fbuf[me]

    for q in range(slabs):
        sl = slice(q * LANES, (q + 1) * LANES)
        s = fresh[0, :, sl]
        s_loc[0, :, sl] = jnp.zeros((128, LANES), BF16)
        for c in range(1, chunks):
            s_loc[c, :, sl] = s.astype(BF16)
            s = grow[c * CH + CH - 1 : c * CH + CH, sl] * s + fresh[c, :, sl]

    skip8 = jnp.broadcast_to(skip_ref[...], (8, heads))
    skip_row = dot(expand(skip8), spread[...])
    lane = lax.broadcasted_iota(jnp.int32, (1, LANES), 1)
    front = jnp.where(lane < LANES // 2, 1.0, 0.0).astype(BF16)
    back_half = jnp.where(lane < LANES // 2, 0.0, 1.0).astype(BF16)

    def local(c, _):
        at = pl.ds(pl.multiple_of(c * CH, CH), CH)
        qc = qs[at, :]
        scores = jnp.where(low_b <= low_a, dot(qc, keys_t[c]), 0.0)
        for q in range(slabs):
            sl = slice(q * LANES, (q + 1) * LANES)
            mixes = []
            for h in (2 * q, 2 * q + 1):
                gap = ct[c, :, h : h + 1] - cs[c, h : h + 1, :]
                mixes.append((jnp.exp(jnp.minimum(gap, 0.0)) * scores).astype(BF16))
            v = vals[at, sl]
            rhs = jnp.concatenate([v * front, v * back_half], axis=0)
            o = dot(jnp.concatenate(mixes, axis=1), rhs)
            g = grow[at, sl]
            o = o + g * dot(qc, s_loc[c, :, sl])
            mixed[at, sl] = o + skip_row[0:1, sl] * v.astype(F32)
            grow[at, sl] = g * ap[c, 0:1, sl]
        return 0

    lax.fori_loop(0, chunks, local, 0)

    def await_f(i, _):
        b = lax.rem(me + i, n_seq)
        a_copy(b, b).wait_recv()
        f_copy(b, b).wait_recv()
        return 0

    lax.fori_loop(1, n_seq, await_f, 0)
    state = jnp.zeros((seg // 8, 8, LANES), F32)
    for b in range(n_seq):
        sbuf[b] = state.astype(BF16).reshape(seg, LANES)
        state = ra[b][None] * state + rf[b].astype(F32).reshape(seg // 8, 8, LANES)
    far_first(s_copy)
    s_in[me] = sbuf[me]

    gate_load.wait()

    def gate(i, _):
        at = pl.ds(pl.multiple_of(i * 16, 16), 16)
        s = silu(gates[at, :].astype(F32))
        mixed[at, :] = mixed[at, :] * s
        grow[at, :] = grow[at, :] * s
        return 0

    lax.fori_loop(0, rows // 16, gate, 0)
    for load in w_loads:
        load.wait()
    for k in range(4):
        w_copy(k).wait_recv()

    def await_s(i, _):
        b = lax.rem(me + i, n_seq)
        s_copy(b, b).wait_recv()
        return 0

    lax.fori_loop(1, n_seq, await_s, 0)

    def y_copy(p):
        return pltpu.make_async_remote_copy(
            src_ref=y.at[p],
            dst_ref=y_mate.at[p],
            send_sem=y_s.at[p],
            recv_sem=y_r.at[p],
            device_id={"tp": mate},
            device_id_type=MESH,
        )

    def finish_rows(p):
        at = slice(p * quarter, (p + 1) * quarter)
        qm = qs[at, :]
        total = jnp.zeros((quarter, LANES), F32)
        for j in range(width // 256):
            pair = [
                s_in[(2 * j + i) * split : (2 * j + i + 1) * split].reshape(128, LANES)
                for i in range(2)
            ]
            t = dot(qm, jnp.concatenate(pair, axis=1))
            sl = slice(j * 256, (j + 1) * 256)
            x = mixed[at, sl] + grow[at, sl] * t
            mixed[at, sl] = x
            total = total + x[:, :LANES] * x[:, :LANES] + x[:, LANES:] * x[:, LANES:]
        scale = lax.rsqrt(jnp.sum(total, axis=1, keepdims=True) * (1.0 / width) + EPS)
        for j in range(slabs):
            sl = slice(j * LANES, (j + 1) * LANES)
            y[p, :, sl] = (mixed[at, sl] * scale * gain_ref[:, sl]).astype(BF16)
        y_copy(p).start()

    def x_copy(send, recv, ss, rs, m, way):
        return pltpu.make_async_remote_copy(
            src_ref=send.at[m, way],
            dst_ref=recv.at[m, way],
            send_sem=ss.at[m, way],
            recv_sem=rs.at[m, way],
            device_id={"tp": ahead if way == 0 else behind},
            device_id_type=MESH,
        )

    def h_copy(m, way):
        return x_copy(h_send, h_recv, h_s, h_r, m, way)

    def d_copy(m, way):
        return x_copy(d_send, d_recv, d_s, d_r, m, way)

    def c_copy(m, way):
        return x_copy(c_send, c_recv, c_s, c_r, m, way)

    def chip_sum(m, k):
        rows_own = y[2 * m : 2 * m + 2].reshape(half, width)
        rows_mate = y_mate[2 * m : 2 * m + 2].reshape(half, width)
        return dot(rows_own, w_own[k]) + dot(rows_mate, w_mate[k])

    for p in range(4):
        finish_rows(p)
    for p in range(4):
        first[p] = dot(y[p], w_own[0])
    for p in range(4):
        y_copy(p).wait_recv()
        h_send[p // 2, p % 2] = (first[p] + dot(y_mate[p], w_mate[0])).astype(BF16)
        h_copy(p // 2, p % 2).start()
    for m in range(2):
        for way in range(2):
            total = chip_sum(m, 1 + way)
            parts = total[:quarter], total[quarter:]
            d_send[m, way] = parts[1 - way].astype(BF16)
            d_copy(m, way).start()
            join[m, way] = parts[way]
    for m in range(2):
        own[m] = chip_sum(m, 3)
    for m in range(2):
        for way in range(2):
            h_copy(m, way).wait_recv()
            c_send[m, way] = (join[m, way] + h_recv[m, way].astype(F32)).astype(BF16)
            c_copy(m, way).start()
    for m in range(2):
        for way in range(2):
            d_copy(m, 1 - way).wait_recv()
            c_copy(m, way).wait_recv()
            lo = way * quarter
            total = own[m, lo : lo + quarter, :]
            total = total + d_recv[m, 1 - way].astype(F32) + c_recv[m, way].astype(F32)
            out_ref[m * half + lo : m * half + lo + quarter, :] = total.astype(BF16)

    for halo in halos:
        halo.wait_send()

    def drain(i, _):
        b = lax.rem(me + i, n_seq)
        a_copy(b, me).wait_send()
        f_copy(b, me).wait_send()
        s_copy(b, me).wait_send()
        return 0

    lax.fori_loop(1, n_seq, drain, 0)
    for k in range(4):
        w_copy(k).wait_send()
        y_copy(k).wait_send()
    for m in range(2):
        for way in range(2):
            h_copy(m, way).wait_send()
            d_copy(m, way).wait_send()
            c_copy(m, way).wait_send()


def shards(
    n_seq,
    values_in,
    gates_in,
    keys_in,
    queries_in,
    log_decay,
    conv_values,
    bias_values,
    conv_keys,
    bias_keys,
    conv_queries,
    bias_queries,
    skip_scale,
    norm_gain,
    out_weight,
):
    rows, width = values_in.shape
    heads = log_decay.shape[0]
    chunks = rows // CH
    slabs = width // LANES
    seg = 128 * slabs // n_seq
    half, quarter = rows // 2, rows // 4
    depth, full = out_weight.shape
    cols = full // 8
    hbm = pl.BlockSpec(memory_space=pl.ANY)
    dma = pltpu.SemaphoreType.DMA
    args = (
        values_in,
        gates_in,
        keys_in,
        queries_in,
        log_decay,
        conv_values,
        bias_values[None],
        conv_keys,
        bias_keys[None],
        conv_queries,
        bias_queries[None],
        skip_scale[None],
        norm_gain[None],
        out_weight,
    )
    return pl.pallas_call(
        functools.partial(kernel, n_seq),
        out_shape=jax.ShapeDtypeStruct((rows, cols), BF16),
        in_specs=[hbm] * len(args),
        out_specs=pl.BlockSpec(memory_space=pltpu.VMEM),
        scratch_shapes=[pltpu.VMEM(a.shape, a.dtype) for a in args[4:13]]
        + [
            pltpu.VMEM((rows + PAD, width + 256), BF16),
            pltpu.VMEM((PAD, width + 256), BF16),
            pltpu.VMEM((rows, width), BF16),
            pltpu.VMEM((4, depth, cols), BF16),
            pltpu.VMEM((4, depth, cols), BF16),
            pltpu.VMEM((2 * heads, width), BF16),
            pltpu.VMEM((3 * CH, CH + PAD), BF16),
            pltpu.VMEM((3 * PAD, 2 * PAD), BF16),
            pltpu.VMEM((chunks, CH, heads), F32),
            pltpu.VMEM((chunks, heads, CH), F32),
            pltpu.VMEM((rows, width), F32),
            pltpu.VMEM((rows, width), F32),
            pltpu.VMEM((chunks, 8, width), F32),
            pltpu.VMEM((rows, width), BF16),
            pltpu.VMEM((CH, width), BF16),
            pltpu.VMEM((CH, 128), BF16),
            pltpu.VMEM((chunks, 128, CH), BF16),
            pltpu.VMEM((rows, 128), BF16),
            pltpu.VMEM((chunks, 128, width), F32),
            pltpu.VMEM((128, width), F32),
            pltpu.VMEM((chunks, 128, width), BF16),
            pltpu.VMEM((rows, width), F32),
            pltpu.VMEM((slabs, 8, LANES), F32),
            pltpu.VMEM((n_seq, 8, LANES), F32),
            pltpu.VMEM((n_seq, seg, LANES), BF16),
            pltpu.VMEM((n_seq, seg, LANES), BF16),
            pltpu.VMEM((n_seq, seg, LANES), BF16),
            pltpu.VMEM((n_seq, seg, LANES), BF16),
            pltpu.VMEM((4, quarter, width), BF16),
            pltpu.VMEM((4, quarter, width), BF16),
            pltpu.VMEM((4, quarter, cols), F32),
            pltpu.VMEM((2, half, cols), F32),
            pltpu.VMEM((2, 2, quarter, cols), F32),
        ]
        + [pltpu.VMEM((2, 2, quarter, cols), BF16)] * 6
        + [dma((9,)), dma((4,)), dma((4,)), dma((4,)), dma((4,)), dma((3,)), dma((3,))]
        + [dma((n_seq,))] * 6
        + [dma((4,))] * 2
        + [dma((2, 2))] * 6,
        compiler_params=pltpu.CompilerParams(
            collective_id=0, has_side_effects=True, vmem_limit_bytes=48 * 2**20
        ),
        name="mixer",
    )(*[pltpu.with_memory_space_constraint(a, pltpu.HBM) for a in args])


def solution(mesh):
    placed = (
        P("seq", "tp"),
        P("seq", "tp"),
        P("seq", "tp"),
        P("seq", "tp"),
        P("tp", "seq"),
        P(None, "tp"),
        P("tp"),
        P(None, "tp"),
        P("tp"),
        P(None, "tp"),
        P("tp"),
        P("tp"),
        P("tp"),
        P("tp", None),
    )
    return jax.shard_map(
        functools.partial(shards, mesh.shape["seq"]),
        mesh=mesh,
        in_specs=placed,
        out_specs=P("seq", "tp"),
        check_vma=False,
    )
```

```python
import functools

import jax
import jax.numpy as jnp
from jax import lax
from jax.experimental import pallas as pl
from jax.experimental.pallas import tpu as pltpu
from jax.sharding import PartitionSpec as P

MESH = pl.DeviceIdType.MESH
F32 = jnp.float32
BF16 = jnp.bfloat16
EPS = 1e-05
CH = 128
PAD = 16
LANES = 128
ROW = 8


def dot(a, b):
    return jnp.dot(a, b, preferred_element_type=F32)


def silu(v):
    h = 0.5 * v
    return h + h * jnp.tanh(h)


def parts_of(x):
    hi = x.astype(BF16).astype(F32)
    rest = x - hi
    mid = rest.astype(BF16).astype(F32)
    return hi, mid, rest - mid


def kernel(
    n_seq,
    v_hbm,
    g_hbm,
    k_hbm,
    q_hbm,
    log_hbm,
    cv_hbm,
    bv_hbm,
    ck_hbm,
    bk_hbm,
    cq_hbm,
    bq_hbm,
    skip_hbm,
    gain_hbm,
    w_hbm,
    out_ref,
    log_ref,
    cv_ref,
    bv_ref,
    ck_ref,
    bk_ref,
    cq_ref,
    bq_ref,
    skip_ref,
    gain_ref,
    xpad,
    edge,
    gates,
    w_own,
    w_mate,
    spread,
    shift_top,
    ct,
    cs,
    grow,
    rem,
    dec,
    ap,
    vals,
    vw,
    keys0,
    keys_t,
    qs,
    fresh,
    rest,
    s_loc,
    mixed,
    abuf,
    ra,
    fbuf,
    rf,
    sbuf,
    s_in,
    y,
    y_mate,
    first,
    own,
    join,
    h_send,
    h_recv,
    d_send,
    d_recv,
    c_send,
    c_recv,
    small_sem,
    in_sem,
    w_sem,
    wx_s,
    wx_r,
    halo_s,
    halo_r,
    a_s,
    a_r,
    b_s,
    b_r,
    f_s,
    f_r,
    s_s,
    s_r,
    y_s,
    y_r,
    h_s,
    h_r,
    d_s,
    d_r,
    c_s,
    c_r,
):
    rows, width = v_hbm.shape
    heads = log_ref.shape[0]
    hops = sorted(
        ((dy, dz) for dy in range(n_seq // ROW) for dz in range(ROW) if dy or dz),
        key=lambda o: -min(o[0], n_seq // ROW - o[0]) - min(o[1], ROW - o[1]),
    )
    chunks = rows // CH
    slabs = width // LANES
    split = n_seq // slabs
    seg = 128 // split
    half = rows // 2
    quarter = half // 2
    tp_size = lax.axis_size("tp")
    me = lax.axis_index("seq")
    tp = lax.axis_index("tp")
    core = lax.rem(tp, 2)
    mate = tp + 1 - 2 * core
    ahead = lax.rem(tp + 2, tp_size)
    behind = lax.rem(tp + tp_size - 2, tp_size)
    far = lax.rem(tp + 4, tp_size)

    barrier = pltpu.get_barrier_semaphore()

    def greet(i, _):
        pl.semaphore_signal(
            barrier, inc=1, device_id={"seq": lax.rem(me + i, n_seq)}, device_id_type=MESH
        )
        return 0

    lax.fori_loop(1, n_seq, greet, 0)
    for other in (mate, ahead, behind):
        pl.semaphore_signal(barrier, inc=1, device_id={"tp": other}, device_id_type=MESH)

    smalls = [
        pltpu.make_async_copy(src, dst, small_sem.at[i])
        for i, (src, dst) in enumerate(
            (
                (log_hbm, log_ref),
                (cv_hbm, cv_ref),
                (bv_hbm, bv_ref),
                (ck_hbm, ck_ref),
                (bk_hbm, bk_ref),
                (cq_hbm, cq_ref),
                (bq_hbm, bq_ref),
                (skip_hbm, skip_ref),
                (gain_hbm, gain_ref),
            )
        )
    ]
    loads = [
        pltpu.make_async_copy(v_hbm, xpad.at[pl.ds(PAD, rows), pl.ds(0, width)], in_sem.at[0]),
        pltpu.make_async_copy(
            k_hbm, xpad.at[pl.ds(PAD, rows), pl.ds(width, 128)], in_sem.at[1]
        ),
        pltpu.make_async_copy(
            q_hbm, xpad.at[pl.ds(PAD, rows), pl.ds(width + 128, 128)], in_sem.at[2]
        ),
    ]
    gate_load = pltpu.make_async_copy(g_hbm, gates, in_sem.at[3])
    for load in smalls + loads:
        load.start()
    cols = w_hbm.shape[1] // tp_size

    def w_part(k, side):
        chip = (far, ahead, behind, tp)[k] - core
        return w_hbm.at[:, pl.ds(pl.multiple_of((chip + side) * cols, cols), cols)]

    w_loads = [
        pltpu.make_async_copy(w_part(k, core), w_own.at[k], w_sem.at[k]) for k in range(4)
    ]

    def w_copy(k):
        return pltpu.make_async_remote_copy(
            src_ref=w_part(k, 1 - core),
            dst_ref=w_mate.at[k],
            send_sem=wx_s.at[k],
            recv_sem=wx_r.at[k],
            device_id={"tp": mate},
            device_id_type=MESH,
        )

    xpad[0:PAD, :] = jnp.zeros((PAD, xpad.shape[1]), BF16)
    for ref, span in ((shift_top, PAD),):
        out_row = lax.broadcasted_iota(jnp.int32, ref.shape, 0)
        in_row = lax.broadcasted_iota(jnp.int32, ref.shape, 1)
        hit = out_row == -1
        for back in range(1, 4):
            base = (back - 1) * span
            here = (out_row >= base) & (out_row < base + span)
            hit = hit | (here & (in_row == out_row - base + PAD - back))
        ref[...] = jnp.where(hit, 1.0, 0.0).astype(BF16)

    lane_head = lax.broadcasted_iota(jnp.int32, (2 * heads, width), 1) // (width // heads)
    row_head = lax.broadcasted_iota(jnp.int32, (2 * heads, width), 0)
    row_head = jnp.where(row_head >= heads, row_head - heads, row_head)
    spread[...] = jnp.where(lane_head == row_head, 1.0, 0.0).astype(BF16)

    def expand(x):
        hi = x.astype(BF16).astype(F32)
        return jnp.concatenate([hi, x - hi], axis=1).astype(BF16)

    low_a = lax.broadcasted_iota(jnp.int32, (CH, CH), 0)
    low_b = lax.broadcasted_iota(jnp.int32, (CH, CH), 1)
    lower = jnp.where(low_b <= low_a, 1.0, 0.0)
    lower3 = jnp.concatenate([lower] * 3, axis=1).astype(BF16)
    upper = jnp.where(low_a <= low_b, 1.0, 0.0)
    upper3 = jnp.concatenate([upper] * 3, axis=0).astype(BF16)

    def decay(c, _):
        at = pl.ds(pl.multiple_of(c * CH, CH), CH)
        logs = jnp.concatenate(parts_of(log_ref[:, at]), axis=1).astype(BF16)
        col = lax.dot_general(lower3, logs, (((1,), (1,)), ((), ())), preferred_element_type=F32)
        ct[c] = col
        cs[c] = dot(logs, upper3)
        last = expand(jnp.exp(col[CH - 8 :, :]))
        r2 = expand(jnp.exp(jnp.minimum(col[CH - 1 : CH, :] - col, 0.0)))
        for j in range(width // 256):
            sl = slice(j * 256, (j + 1) * 256)
            dec[c, :, sl] = dot(last, spread[:, sl])
            rem[at, sl] = dot(r2, spread[:, sl])
        return 0

    smalls[0].wait()
    lax.fori_loop(0, chunks, decay, 0)
    before = jnp.ones((1, width), F32)
    for c in range(chunks):
        ap[c] = jnp.broadcast_to(before, (8, width))
        before = before * dec[c, 7:8, :]
    for q in range(slabs):
        abuf[q : q + 1, :] = before[:, q * LANES : (q + 1) * LANES]
    after = {"seq": lax.rem(me + 1, n_seq)}
    halos = []
    for i, (src, lo, wid) in enumerate(
        ((v_hbm, 0, width), (k_hbm, width, 128), (q_hbm, width + 128, 128))
    ):
        halos.append(
            pltpu.make_async_remote_copy(
                src_ref=src.at[pl.ds(rows - PAD, PAD), :],
                dst_ref=edge.at[:, pl.ds(lo, wid)],
                send_sem=halo_s.at[i],
                recv_sem=halo_r.at[i],
                device_id=after,
                device_id_type=MESH,
            )
        )

    row, col = me // ROW, lax.rem(me, ROW)

    def a_copy(i):
        return pltpu.make_async_remote_copy(
            src_ref=abuf,
            dst_ref=ra.at[me],
            send_sem=a_s.at[i],
            recv_sem=a_r.at[i],
            device_id={"seq": row * ROW + lax.rem(col + i, ROW)},
            device_id_type=MESH,
        )

    def b_copy(i):
        mine = pl.ds(pl.multiple_of(row * ROW, ROW), ROW)
        return pltpu.make_async_remote_copy(
            src_ref=ra.at[mine],
            dst_ref=ra.at[mine],
            send_sem=b_s.at[i],
            recv_sem=b_r.at[i],
            device_id={"seq": lax.rem(row + i, n_seq // ROW) * ROW + col},
            device_id_type=MESH,
        )

    def f_copy(peer, slot):
        return pltpu.make_async_remote_copy(
            src_ref=fbuf.at[peer],
            dst_ref=rf.at[slot],
            send_sem=f_s.at[peer],
            recv_sem=f_r.at[slot],
            device_id={"seq": peer},
            device_id_type=MESH,
        )

    def s_copy(peer, slot):
        return pltpu.make_async_remote_copy(
            src_ref=sbuf.at[peer],
            dst_ref=s_in.at[slot],
            send_sem=s_s.at[peer],
            recv_sem=s_r.at[slot],
            device_id={"seq": peer},
            device_id_type=MESH,
        )

    def taps(x, shifted, span, w_ref, b_ref, sl):
        acc = b_ref[:, sl] + w_ref[3:4, sl] * x.astype(F32)
        for back in range(1, 4):
            acc = acc + w_ref[3 - back : 4 - back, sl] * shifted[(back - 1) * span : back * span]
        return silu(acc).astype(BF16)

    def rolled(window, lo, w_ref, b_ref, sl):
        x = xpad[window, lo : lo + LANES].astype(F32)
        acc = b_ref[:, sl] + w_ref[3:4, sl] * x[PAD:]
        for back in range(1, 4):
            acc = acc + w_ref[3 - back : 4 - back, sl] * pltpu.roll(x, back, axis=0)[PAD:]
        return silu(acc).astype(BF16)

    def conv(c, top):
        at = pl.ds(pl.multiple_of(c * CH, CH), CH)
        window = pl.ds(pl.multiple_of(c * CH, CH), CH + PAD)
        one = slice(0, 128)
        keys = rolled(window, width, ck_ref, bk_ref, one)
        kt = keys.astype(F32).T.astype(BF16)
        keys_t[c] = kt
        if top:
            keys0[...] = keys
        qs[at, :] = rolled(window, width + 128, cq_ref, bq_ref, one)
        for j in range(slabs):
            sl = slice(j * LANES, (j + 1) * LANES)
            v = rolled(window, j * LANES, cv_ref, bv_ref, sl)
            vals[at, sl] = v
            vw[:, sl] = (v.astype(F32) * rem[at, sl]).astype(BF16)
            if top:
                vw[0:PAD, sl] = jnp.zeros((PAD, LANES), BF16)
        for j in range(width // 256):
            sl = slice(j * 256, (j + 1) * 256)
            fresh[c, :, sl] = dot(kt, vw[:, sl])

    for load in smalls[1:] + loads:
        load.wait()
    gate_load.start()
    for load in w_loads:
        load.start()

    def conv_step(i, _):
        conv(chunks - i, False)
        return 0

    lax.fori_loop(1, 3, conv_step, 0)

    pl.semaphore_wait(barrier, n_seq - 1 + 3)
    for halo in halos:
        halo.start()
    for i in range(1, ROW):
        a_copy(i).start()
    ra[me] = abuf[...]
    for k in range(4):
        w_copy(k).start()

    lax.fori_loop(3, chunks, conv_step, 0)
    conv(0, True)
    for q in range(slabs):
        sl = slice(q * LANES, (q + 1) * LANES)
        s = fresh[0, :, sl]
        for c in range(1, chunks):
            s = dec[c, 7:8, sl] * s + fresh[c, :, sl]
        rest[:, sl] = s

    later = jnp.ones((1, width), F32)
    for c in range(1, chunks):
        later = later * dec[c, 7:8, :]
    is_first = me == 0
    for halo in halos:
        halo.wait_recv()
    head = slice(0, PAD)

    def top_rows(sl):
        above = jnp.where(is_first, 0.0, edge[:, sl].astype(F32)).astype(BF16)
        here = xpad[PAD : 2 * PAD, sl]
        return here, dot(shift_top[...], jnp.concatenate([above, here], axis=0))

    x, moved = top_rows(slice(width, width + 256))
    keys0[head, :] = taps(x[:, :128], moved[:, :128], PAD, ck_ref, bk_ref, slice(0, 128))
    qs[head, :] = taps(x[:, 128:], moved[:, 128:], PAD, cq_ref, bq_ref, slice(0, 128))
    kt = keys0[...].astype(F32).T.astype(BF16)
    keys_t[0] = kt
    for j in range(width // 256):
        sl = slice(j * 256, (j + 1) * 256)
        x, moved = top_rows(sl)
        v = taps(x, moved, PAD, cv_ref, bv_ref, sl)
        vals[head, sl] = v
        weighted = (v.astype(F32) * rem[head, sl]).astype(BF16)
        more = dot(kt[:, :PAD], weighted)
        fresh[0, :, sl] = fresh[0, :, sl] + more
        f = (rest[:, sl] + later[:, sl] * more).astype(BF16)
        for i in range(2):
            for r in range(split):
                fbuf[(2 * j + i) * split + r] = f[
                    r * seg : (r + 1) * seg, i * LANES : (i + 1) * LANES
                ]

    def far_first(copy):
        for dy, dz in hops:
            at = lax.rem(me // ROW + dy, n_seq // ROW) * ROW + lax.rem(lax.rem(me, ROW) + dz, ROW)
            copy(at, me).start()

    far_first(f_copy)
    rf[me] = fbuf[me]
    for i in range(1, ROW):
        a_copy(i).wait_recv()
    for i in range(1, n_seq // ROW):
        b_copy(i).start()

    for q in range(slabs):
        sl = slice(q * LANES, (q + 1) * LANES)
        s = fresh[0, :, sl]
        s_loc[0, :, sl] = jnp.zeros((128, LANES), BF16)
        for c in range(1, chunks):
            s_loc[c, :, sl] = s.astype(BF16)
            s = dec[c, 7:8, sl] * s + fresh[c, :, sl]

    skip8 = jnp.broadcast_to(skip_ref[...], (8, heads))
    skip_row = dot(expand(skip8), spread[...])
    lane = lax.broadcasted_iota(jnp.int32, (1, LANES), 1)
    front = jnp.where(lane < LANES // 2, 1.0, 0.0).astype(BF16)
    back_half = jnp.where(lane < LANES // 2, 0.0, 1.0).astype(BF16)

    def local(c, _):
        at = pl.ds(pl.multiple_of(c * CH, CH), CH)
        qc = qs[at, :]
        g2 = expand(jnp.exp(ct[c]))
        scores = jnp.where(low_b <= low_a, dot(qc, keys_t[c]), 0.0)
        for q in range(slabs):
            sl = slice(q * LANES, (q + 1) * LANES)
            mixes = []
            for h in (2 * q, 2 * q + 1):
                gap = ct[c, :, h : h + 1] - cs[c, h : h + 1, :]
                mixes.append((jnp.exp(jnp.minimum(gap, 0.0)) * scores).astype(BF16))
            v = vals[at, sl]
            rhs = jnp.concatenate([v * front, v * back_half], axis=0)
            o = dot(jnp.concatenate(mixes, axis=1), rhs)
            g = dot(g2, spread[:, sl])
            o = o + g * dot(qc, s_loc[c, :, sl])
            mixed[at, sl] = o + skip_row[0:1, sl] * v.astype(F32)
            grow[at, sl] = g * ap[c, 0:1, sl]
        return 0

    lax.fori_loop(0, chunks, local, 0)

    def await_f(i, _):
        b = lax.rem(me + i, n_seq)
        f_copy(b, b).wait_recv()
        return 0

    lax.fori_loop(1, n_seq, await_f, 0)
    for i in range(1, n_seq // ROW):
        b_copy(i).wait_recv()
    state = jnp.zeros((seg // 8, 8, LANES), F32)
    for b in range(n_seq):
        sbuf[b] = state.astype(BF16).reshape(seg, LANES)
        state = ra[b, pl.ds(me // split, 1), :][None] * state + rf[b].astype(F32).reshape(seg // 8, 8, LANES)
    far_first(s_copy)
    s_in[me] = sbuf[me]

    gate_load.wait()

    def gate(i, _):
        at = pl.ds(pl.multiple_of(i * 16, 16), 16)
        s = silu(gates[at, :].astype(F32))
        mixed[at, :] = mixed[at, :] * s
        grow[at, :] = grow[at, :] * s
        return 0

    lax.fori_loop(0, rows // 16, gate, 0)
    for load in w_loads:
        load.wait()
    for k in range(4):
        w_copy(k).wait_recv()

    def await_s(i, _):
        b = lax.rem(me + i, n_seq)
        s_copy(b, b).wait_recv()
        return 0

    lax.fori_loop(1, n_seq, await_s, 0)

    def y_copy(p):
        return pltpu.make_async_remote_copy(
            src_ref=y.at[p],
            dst_ref=y_mate.at[p],
            send_sem=y_s.at[p],
            recv_sem=y_r.at[p],
            device_id={"tp": mate},
            device_id_type=MESH,
        )

    def finish_rows(p):
        at = slice(p * quarter, (p + 1) * quarter)
        qm = qs[at, :]
        total = jnp.zeros((quarter, LANES), F32)
        for j in range(width // 256):
            pair = [
                s_in[(2 * j + i) * split : (2 * j + i + 1) * split].reshape(128, LANES)
                for i in range(2)
            ]
            t = dot(qm, jnp.concatenate(pair, axis=1))
            sl = slice(j * 256, (j + 1) * 256)
            x = mixed[at, sl] + grow[at, sl] * t
            mixed[at, sl] = x
            total = total + x[:, :LANES] * x[:, :LANES] + x[:, LANES:] * x[:, LANES:]
        scale = lax.rsqrt(jnp.sum(total, axis=1, keepdims=True) * (1.0 / width) + EPS)
        for j in range(slabs):
            sl = slice(j * LANES, (j + 1) * LANES)
            y[p, :, sl] = (mixed[at, sl] * scale * gain_ref[:, sl]).astype(BF16)

    def x_copy(send, recv, ss, rs, m, way):
        return pltpu.make_async_remote_copy(
            src_ref=send.at[m, way],
            dst_ref=recv.at[m, way],
            send_sem=ss.at[m, way],
            recv_sem=rs.at[m, way],
            device_id={"tp": ahead if way == 0 else behind},
            device_id_type=MESH,
        )

    def h_copy(m, way):
        return x_copy(h_send, h_recv, h_s, h_r, m, way)

    def d_copy(m, way):
        return x_copy(d_send, d_recv, d_s, d_r, m, way)

    def c_copy(m, way):
        return x_copy(c_send, c_recv, c_s, c_r, m, way)

    def chip_sum(m, k):
        rows_own = y[2 * m : 2 * m + 2].reshape(half, width)
        rows_mate = y_mate[2 * m : 2 * m + 2].reshape(half, width)
        return dot(rows_own, w_own[k]) + dot(rows_mate, w_mate[k])

    for p in range(4):
        finish_rows(p)
        if p < 2:
            y_copy(p).start()
    for p in range(4):
        first[p] = dot(y[p], w_own[0])
    for p in range(4):
        if p == 0:
            y_copy(0).wait_send()
            y_copy(1).wait_send()
            y_copy(2).start()
            y_copy(3).start()
        y_copy(p).wait_recv()
        h_send[p // 2, p % 2] = (first[p] + dot(y_mate[p], w_mate[0])).astype(BF16)
        h_copy(p // 2, p % 2).start()
    for m in range(2):
        for way in range(2):
            total = chip_sum(m, 1 + way)
            parts = total[:quarter], total[quarter:]
            d_send[m, way] = parts[1 - way].astype(BF16)
            d_copy(m, way).start()
            join[m, way] = parts[way]
    for m in range(2):
        own[m] = chip_sum(m, 3)
    for m in range(2):
        for way in range(2):
            h_copy(m, way).wait_recv()
            c_send[m, way] = (join[m, way] + h_recv[m, way].astype(F32)).astype(BF16)
            c_copy(m, way).start()
    for m in range(2):
        for way in range(2):
            d_copy(m, 1 - way).wait_recv()
            c_copy(m, way).wait_recv()
            lo = way * quarter
            total = own[m, lo : lo + quarter, :]
            total = total + d_recv[m, 1 - way].astype(F32) + c_recv[m, way].astype(F32)
            out_ref[m * half + lo : m * half + lo + quarter, :] = total.astype(BF16)

    for halo in halos:
        halo.wait_send()

    def drain(i, _):
        b = lax.rem(me + i, n_seq)
        f_copy(b, me).wait_send()
        s_copy(b, me).wait_send()
        return 0

    lax.fori_loop(1, n_seq, drain, 0)
    for i in range(1, ROW):
        a_copy(i).wait_send()
    for i in range(1, n_seq // ROW):
        b_copy(i).wait_send()
    for k in range(4):
        w_copy(k).wait_send()
    for p in range(2, 4):
        y_copy(p).wait_send()
    for m in range(2):
        for way in range(2):
            h_copy(m, way).wait_send()
            d_copy(m, way).wait_send()
            c_copy(m, way).wait_send()


def shards(
    n_seq,
    values_in,
    gates_in,
    keys_in,
    queries_in,
    log_decay,
    conv_values,
    bias_values,
    conv_keys,
    bias_keys,
    conv_queries,
    bias_queries,
    skip_scale,
    norm_gain,
    out_weight,
):
    rows, width = values_in.shape
    heads = log_decay.shape[0]
    chunks = rows // CH
    slabs = width // LANES
    seg = 128 * slabs // n_seq
    half, quarter = rows // 2, rows // 4
    depth, full = out_weight.shape
    cols = full // 8
    hbm = pl.BlockSpec(memory_space=pl.ANY)
    dma = pltpu.SemaphoreType.DMA
    args = (
        values_in,
        gates_in,
        keys_in,
        queries_in,
        log_decay,
        conv_values,
        bias_values[None],
        conv_keys,
        bias_keys[None],
        conv_queries,
        bias_queries[None],
        skip_scale[None],
        norm_gain[None],
        out_weight,
    )
    return pl.pallas_call(
        functools.partial(kernel, n_seq),
        out_shape=jax.ShapeDtypeStruct((rows, cols), BF16),
        in_specs=[hbm] * len(args),
        out_specs=pl.BlockSpec(memory_space=pltpu.VMEM),
        scratch_shapes=[pltpu.VMEM(a.shape, a.dtype) for a in args[4:13]]
        + [
            pltpu.VMEM((rows + PAD, width + 256), BF16),
            pltpu.VMEM((PAD, width + 256), BF16),
            pltpu.VMEM((rows, width), BF16),
            pltpu.VMEM((4, depth, cols), BF16),
            pltpu.VMEM((4, depth, cols), BF16),
            pltpu.VMEM((2 * heads, width), BF16),
            pltpu.VMEM((3 * PAD, 2 * PAD), BF16),
            pltpu.VMEM((chunks, CH, heads), F32),
            pltpu.VMEM((chunks, heads, CH), F32),
            pltpu.VMEM((rows, width), F32),
            pltpu.VMEM((rows, width), F32),
            pltpu.VMEM((chunks, 8, width), F32),
            pltpu.VMEM((chunks, 8, width), F32),
            pltpu.VMEM((rows, width), BF16),
            pltpu.VMEM((CH, width), BF16),
            pltpu.VMEM((CH, 128), BF16),
            pltpu.VMEM((chunks, 128, CH), BF16),
            pltpu.VMEM((rows, 128), BF16),
            pltpu.VMEM((chunks, 128, width), F32),
            pltpu.VMEM((128, width), F32),
            pltpu.VMEM((chunks, 128, width), BF16),
            pltpu.VMEM((rows, width), F32),
            pltpu.VMEM((slabs, LANES), F32),
            pltpu.VMEM((n_seq, slabs, LANES), F32),
            pltpu.VMEM((n_seq, seg, LANES), BF16),
            pltpu.VMEM((n_seq, seg, LANES), BF16),
            pltpu.VMEM((n_seq, seg, LANES), BF16),
            pltpu.VMEM((n_seq, seg, LANES), BF16),
            pltpu.VMEM((4, quarter, width), BF16),
            pltpu.VMEM((4, quarter, width), BF16),
            pltpu.VMEM((4, quarter, cols), F32),
            pltpu.VMEM((2, half, cols), F32),
            pltpu.VMEM((2, 2, quarter, cols), F32),
        ]
        + [pltpu.VMEM((2, 2, quarter, cols), BF16)] * 6
        + [dma((9,)), dma((4,)), dma((4,)), dma((4,)), dma((4,)), dma((3,)), dma((3,))]
        + [dma((ROW,))] * 2
        + [dma((n_seq // ROW,))] * 2
        + [dma((n_seq,))] * 4
        + [dma((4,))] * 2
        + [dma((2, 2))] * 6,
        compiler_params=pltpu.CompilerParams(
            collective_id=0, has_side_effects=True, vmem_limit_bytes=48 * 2**20
        ),
        name="mixer",
    )(*[pltpu.with_memory_space_constraint(a, pltpu.HBM) for a in args])


def solution(mesh):
    placed = (
        P("seq", "tp"),
        P("seq", "tp"),
        P("seq", "tp"),
        P("seq", "tp"),
        P("tp", "seq"),
        P(None, "tp"),
        P("tp"),
        P(None, "tp"),
        P("tp"),
        P(None, "tp"),
        P("tp"),
        P("tp"),
        P("tp"),
        P("tp", None),
    )
    return jax.shard_map(
        functools.partial(shards, mesh.shape["seq"]),
        mesh=mesh,
        in_specs=placed,
        out_specs=P("seq", "tp"),
        check_vma=False,
    )
```

```python
import functools

import jax
import jax.numpy as jnp
from jax import lax
from jax.experimental import pallas as pl
from jax.experimental.pallas import tpu as pltpu
from jax.sharding import PartitionSpec as P

MESH = pl.DeviceIdType.MESH
F32 = jnp.float32
BF16 = jnp.bfloat16
EPS = 1e-05
CH = 128
PAD = 16
LANES = 128
ROW = 8


def dot(a, b):
    return jnp.dot(a, b, preferred_element_type=F32)


def silu(v):
    h = 0.5 * v
    return h + h * jnp.tanh(h)


def parts_of(x):
    hi = x.astype(BF16).astype(F32)
    rest = x - hi
    mid = rest.astype(BF16).astype(F32)
    return hi, mid, rest - mid


def kernel(
    n_seq,
    v_hbm,
    g_hbm,
    k_hbm,
    q_hbm,
    log_hbm,
    cv_hbm,
    bv_hbm,
    ck_hbm,
    bk_hbm,
    cq_hbm,
    bq_hbm,
    skip_hbm,
    gain_hbm,
    w_hbm,
    out_ref,
    log_ref,
    cv_ref,
    bv_ref,
    ck_ref,
    bk_ref,
    cq_ref,
    bq_ref,
    skip_ref,
    gain_ref,
    xpad,
    edge,
    gates,
    w_own,
    w_mate,
    spread,
    shift_top,
    ct,
    cs,
    grow,
    rem,
    dec,
    ap,
    vals,
    vw,
    keys0,
    keys_t,
    qs,
    fresh,
    rest,
    s_loc,
    mixed,
    abuf,
    ra,
    fbuf,
    rf,
    sbuf,
    s_in,
    y,
    y_mate,
    first,
    own,
    join,
    h_send,
    h_recv,
    d_send,
    d_recv,
    c_send,
    c_recv,
    small_sem,
    in_sem,
    w_sem,
    wx_s,
    wx_r,
    halo_s,
    halo_r,
    a_s,
    a_r,
    b_s,
    b_r,
    f_s,
    f_r,
    s_s,
    s_r,
    y_s,
    y_r,
    h_s,
    h_r,
    d_s,
    d_r,
    c_s,
    c_r,
):
    rows, width = v_hbm.shape
    heads = log_ref.shape[0]
    hops = sorted(
        ((dy, dz) for dy in range(n_seq // ROW) for dz in range(ROW) if dy or dz),
        key=lambda o: -min(o[0], n_seq // ROW - o[0]) - min(o[1], ROW - o[1]),
    )
    chunks = rows // CH
    slabs = width // LANES
    split = n_seq // slabs
    seg = 128 // split
    half = rows // 2
    quarter = half // 2
    tp_size = lax.axis_size("tp")
    me = lax.axis_index("seq")
    tp = lax.axis_index("tp")
    core = lax.rem(tp, 2)
    mate = tp + 1 - 2 * core
    ahead = lax.rem(tp + 2, tp_size)
    behind = lax.rem(tp + tp_size - 2, tp_size)
    far = lax.rem(tp + 4, tp_size)

    barrier = pltpu.get_barrier_semaphore()

    def greet(i, _):
        pl.semaphore_signal(
            barrier, inc=1, device_id={"seq": lax.rem(me + i, n_seq)}, device_id_type=MESH
        )
        return 0

    lax.fori_loop(1, n_seq, greet, 0)
    for other in (mate, ahead, behind):
        pl.semaphore_signal(barrier, inc=1, device_id={"tp": other}, device_id_type=MESH)

    smalls = [
        pltpu.make_async_copy(src, dst, small_sem.at[i])
        for i, (src, dst) in enumerate(
            (
                (log_hbm, log_ref),
                (cv_hbm, cv_ref),
                (bv_hbm, bv_ref),
                (ck_hbm, ck_ref),
                (bk_hbm, bk_ref),
                (cq_hbm, cq_ref),
                (bq_hbm, bq_ref),
                (skip_hbm, skip_ref),
                (gain_hbm, gain_ref),
            )
        )
    ]
    loads = [
        pltpu.make_async_copy(v_hbm, xpad.at[pl.ds(PAD, rows), pl.ds(0, width)], in_sem.at[0]),
        pltpu.make_async_copy(
            k_hbm, xpad.at[pl.ds(PAD, rows), pl.ds(width, 128)], in_sem.at[1]
        ),
        pltpu.make_async_copy(
            q_hbm, xpad.at[pl.ds(PAD, rows), pl.ds(width + 128, 128)], in_sem.at[2]
        ),
    ]
    gate_load = pltpu.make_async_copy(g_hbm, gates, in_sem.at[3])
    for load in smalls + loads:
        load.start()
    cols = w_hbm.shape[1] // tp_size

    def w_part(k, side):
        chip = (far, ahead, behind, tp)[k] - core
        return w_hbm.at[:, pl.ds(pl.multiple_of((chip + side) * cols, cols), cols)]

    w_loads = [
        pltpu.make_async_copy(w_part(k, core), w_own.at[k], w_sem.at[k]) for k in range(4)
    ]

    def w_copy(k):
        return pltpu.make_async_remote_copy(
            src_ref=w_part(k, 1 - core),
            dst_ref=w_mate.at[k],
            send_sem=wx_s.at[k],
            recv_sem=wx_r.at[k],
            device_id={"tp": mate},
            device_id_type=MESH,
        )

    xpad[0:PAD, :] = jnp.zeros((PAD, xpad.shape[1]), BF16)
    for ref, span in ((shift_top, PAD),):
        out_row = lax.broadcasted_iota(jnp.int32, ref.shape, 0)
        in_row = lax.broadcasted_iota(jnp.int32, ref.shape, 1)
        hit = out_row == -1
        for back in range(1, 4):
            base = (back - 1) * span
            here = (out_row >= base) & (out_row < base + span)
            hit = hit | (here & (in_row == out_row - base + PAD - back))
        ref[...] = jnp.where(hit, 1.0, 0.0).astype(BF16)

    lane_head = lax.broadcasted_iota(jnp.int32, (2 * heads, width), 1) // (width // heads)
    row_head = lax.broadcasted_iota(jnp.int32, (2 * heads, width), 0)
    row_head = jnp.where(row_head >= heads, row_head - heads, row_head)
    spread[...] = jnp.where(lane_head == row_head, 1.0, 0.0).astype(BF16)

    def expand(x):
        hi = x.astype(BF16).astype(F32)
        return jnp.concatenate([hi, x - hi], axis=1).astype(BF16)

    low_a = lax.broadcasted_iota(jnp.int32, (CH, CH), 0)
    low_b = lax.broadcasted_iota(jnp.int32, (CH, CH), 1)
    lower = jnp.where(low_b <= low_a, 1.0, 0.0)
    lower3 = jnp.concatenate([lower] * 3, axis=1).astype(BF16)
    upper = jnp.where(low_a <= low_b, 1.0, 0.0)
    upper3 = jnp.concatenate([upper] * 3, axis=0).astype(BF16)

    def decay(c, _):
        at = pl.ds(pl.multiple_of(c * CH, CH), CH)
        logs = jnp.concatenate(parts_of(log_ref[:, at]), axis=1).astype(BF16)
        col = lax.dot_general(lower3, logs, (((1,), (1,)), ((), ())), preferred_element_type=F32)
        ct[c] = col
        cs[c] = dot(logs, upper3)
        last = expand(jnp.exp(col[CH - 8 :, :]))
        r2 = expand(jnp.exp(jnp.minimum(col[CH - 1 : CH, :] - col, 0.0)))
        for j in range(width // 256):
            sl = slice(j * 256, (j + 1) * 256)
            dec[c, :, sl] = dot(last, spread[:, sl])
            rem[at, sl] = dot(r2, spread[:, sl])
        return 0

    smalls[0].wait()
    lax.fori_loop(0, chunks, decay, 0)
    before = jnp.ones((1, width), F32)
    for c in range(chunks):
        ap[c] = jnp.broadcast_to(before, (8, width))
        before = before * dec[c, 7:8, :]
    for q in range(slabs):
        abuf[q : q + 1, :] = before[:, q * LANES : (q + 1) * LANES]
    after = {"seq": lax.rem(me + 1, n_seq)}
    halos = []
    for i, (src, lo, wid) in enumerate(
        ((v_hbm, 0, width), (k_hbm, width, 128), (q_hbm, width + 128, 128))
    ):
        halos.append(
            pltpu.make_async_remote_copy(
                src_ref=src.at[pl.ds(rows - PAD, PAD), :],
                dst_ref=edge.at[:, pl.ds(lo, wid)],
                send_sem=halo_s.at[i],
                recv_sem=halo_r.at[i],
                device_id=after,
                device_id_type=MESH,
            )
        )

    row, col = me // ROW, lax.rem(me, ROW)

    def a_copy(i):
        return pltpu.make_async_remote_copy(
            src_ref=abuf,
            dst_ref=ra.at[me],
            send_sem=a_s.at[i],
            recv_sem=a_r.at[i],
            device_id={"seq": row * ROW + lax.rem(col + i, ROW)},
            device_id_type=MESH,
        )

    def b_copy(i):
        mine = pl.ds(pl.multiple_of(row * ROW, ROW), ROW)
        return pltpu.make_async_remote_copy(
            src_ref=ra.at[mine],
            dst_ref=ra.at[mine],
            send_sem=b_s.at[i],
            recv_sem=b_r.at[i],
            device_id={"seq": lax.rem(row + i, n_seq // ROW) * ROW + col},
            device_id_type=MESH,
        )

    def f_copy(peer, slot):
        return pltpu.make_async_remote_copy(
            src_ref=fbuf.at[peer],
            dst_ref=rf.at[slot],
            send_sem=f_s.at[peer],
            recv_sem=f_r.at[slot],
            device_id={"seq": peer},
            device_id_type=MESH,
        )

    def s_copy(peer, slot):
        return pltpu.make_async_remote_copy(
            src_ref=sbuf.at[peer],
            dst_ref=s_in.at[slot],
            send_sem=s_s.at[peer],
            recv_sem=s_r.at[slot],
            device_id={"seq": peer},
            device_id_type=MESH,
        )

    def taps(x, shifted, span, w_ref, b_ref, sl):
        acc = b_ref[:, sl] + w_ref[3:4, sl] * x.astype(F32)
        for back in range(1, 4):
            acc = acc + w_ref[3 - back : 4 - back, sl] * shifted[(back - 1) * span : back * span]
        return silu(acc).astype(BF16)

    def rolled(window, lo, w_ref, b_ref, sl):
        x = xpad[window, lo : lo + LANES].astype(F32)
        w = 0.5 * w_ref[:, sl]
        acc = 0.5 * b_ref[:, sl] + w[3:4] * x[PAD:]
        for back in range(1, 4):
            acc = acc + w[3 - back : 4 - back] * pltpu.roll(x, back, axis=0)[PAD:]
        return (acc + acc * jnp.tanh(acc)).astype(BF16)

    def conv(c, top):
        at = pl.ds(pl.multiple_of(c * CH, CH), CH)
        window = pl.ds(pl.multiple_of(c * CH, CH), CH + PAD)
        one = slice(0, 128)
        keys = rolled(window, width, ck_ref, bk_ref, one)
        kt = keys.astype(F32).T.astype(BF16)
        keys_t[c] = kt
        if top:
            keys0[...] = keys
        for j in range(slabs):
            sl = slice(j * LANES, (j + 1) * LANES)
            v = rolled(window, j * LANES, cv_ref, bv_ref, sl)
            vals[at, sl] = v
            vw[:, sl] = (v.astype(F32) * rem[at, sl]).astype(BF16)
            if top:
                vw[0:PAD, sl] = jnp.zeros((PAD, LANES), BF16)
        for j in range(width // 256):
            sl = slice(j * 256, (j + 1) * 256)
            fresh[c, :, sl] = dot(kt, vw[:, sl])

    for load in smalls[1:] + loads:
        load.wait()
    gate_load.start()
    for load in w_loads:
        load.start()

    def conv_step(i, _):
        conv(chunks - i, False)
        return 0


    pl.semaphore_wait(barrier, n_seq - 1 + 3)
    for halo in halos:
        halo.start()
    for i in range(1, ROW):
        a_copy(i).start()
    ra[me] = abuf[...]
    lax.fori_loop(1, chunks, conv_step, 0)
    conv(0, True)
    for q in range(slabs):
        sl = slice(q * LANES, (q + 1) * LANES)
        s = fresh[0, :, sl]
        for c in range(1, chunks):
            s = dec[c, 7:8, sl] * s + fresh[c, :, sl]
        rest[:, sl] = s

    later = jnp.ones((1, width), F32)
    for c in range(1, chunks):
        later = later * dec[c, 7:8, :]
    is_first = me == 0
    for halo in halos:
        halo.wait_recv()
    head = slice(0, PAD)

    def top_rows(sl):
        above = jnp.where(is_first, 0.0, edge[:, sl].astype(F32)).astype(BF16)
        here = xpad[PAD : 2 * PAD, sl]
        return here, dot(shift_top[...], jnp.concatenate([above, here], axis=0))

    x_top, moved_top = top_rows(slice(width, width + 256))
    keys0[head, :] = taps(
        x_top[:, :128], moved_top[:, :128], PAD, ck_ref, bk_ref, slice(0, 128)
    )
    kt = keys0[...].astype(F32).T.astype(BF16)
    keys_t[0] = kt
    for j in range(width // 256):
        sl = slice(j * 256, (j + 1) * 256)
        x, moved = top_rows(sl)
        v = taps(x, moved, PAD, cv_ref, bv_ref, sl)
        vals[head, sl] = v
        weighted = (v.astype(F32) * rem[head, sl]).astype(BF16)
        more = dot(kt[:, :PAD], weighted)
        fresh[0, :, sl] = fresh[0, :, sl] + more
        f = (rest[:, sl] + later[:, sl] * more).astype(BF16)
        for i in range(2):
            for r in range(split):
                fbuf[(2 * j + i) * split + r] = f[
                    r * seg : (r + 1) * seg, i * LANES : (i + 1) * LANES
                ]

    def far_first(copy):
        for dy, dz in hops:
            at = lax.rem(me // ROW + dy, n_seq // ROW) * ROW + lax.rem(lax.rem(me, ROW) + dz, ROW)
            copy(at, me).start()

    far_first(f_copy)
    rf[me] = fbuf[me]
    for k in range(4):
        w_copy(k).start()

    def query(c, _):
        at = pl.ds(pl.multiple_of(c * CH, CH), CH)
        window = pl.ds(pl.multiple_of(c * CH, CH), CH + PAD)
        qs[at, :] = rolled(window, width + 128, cq_ref, bq_ref, slice(0, 128))
        return 0

    lax.fori_loop(0, chunks, query, 0)
    qs[head, :] = taps(
        x_top[:, 128:], moved_top[:, 128:], PAD, cq_ref, bq_ref, slice(0, 128)
    )
    for i in range(1, ROW):
        a_copy(i).wait_recv()
    for i in range(1, n_seq // ROW):
        b_copy(i).start()

    for q in range(slabs):
        sl = slice(q * LANES, (q + 1) * LANES)
        s = fresh[0, :, sl]
        s_loc[0, :, sl] = jnp.zeros((128, LANES), BF16)
        for c in range(1, chunks):
            s_loc[c, :, sl] = s.astype(BF16)
            s = dec[c, 7:8, sl] * s + fresh[c, :, sl]

    skip8 = jnp.broadcast_to(skip_ref[...], (8, heads))
    skip_row = dot(expand(skip8), spread[...])
    lane = lax.broadcasted_iota(jnp.int32, (1, LANES), 1)
    front = jnp.where(lane < LANES // 2, 1.0, 0.0).astype(BF16)
    back_half = jnp.where(lane < LANES // 2, 0.0, 1.0).astype(BF16)

    def local(c, _):
        at = pl.ds(pl.multiple_of(c * CH, CH), CH)
        qc = qs[at, :]
        g2 = expand(jnp.exp(ct[c]))
        scores = jnp.where(low_b <= low_a, dot(qc, keys_t[c]), 0.0)
        for q in range(slabs):
            sl = slice(q * LANES, (q + 1) * LANES)
            mixes = []
            for h in (2 * q, 2 * q + 1):
                gap = ct[c, :, h : h + 1] - cs[c, h : h + 1, :]
                mixes.append((jnp.exp(jnp.minimum(gap, 0.0)) * scores).astype(BF16))
            v = vals[at, sl]
            rhs = jnp.concatenate([v * front, v * back_half], axis=0)
            o = dot(jnp.concatenate(mixes, axis=1), rhs)
            g = dot(g2, spread[:, sl])
            o = o + g * dot(qc, s_loc[c, :, sl])
            mixed[at, sl] = o + skip_row[0:1, sl] * v.astype(F32)
            grow[at, sl] = g * ap[c, 0:1, sl]
        return 0

    lax.fori_loop(0, chunks, local, 0)

    def await_f(i, _):
        b = lax.rem(me + i, n_seq)
        f_copy(b, b).wait_recv()
        return 0

    lax.fori_loop(1, n_seq, await_f, 0)
    for i in range(1, n_seq // ROW):
        b_copy(i).wait_recv()
    state = jnp.zeros((seg // 8, 8, LANES), F32)
    for b in range(n_seq):
        sbuf[b] = state.astype(BF16).reshape(seg, LANES)
        state = ra[b, pl.ds(me // split, 1), :][None] * state + rf[b].astype(F32).reshape(seg // 8, 8, LANES)
    far_first(s_copy)
    s_in[me] = sbuf[me]

    gate_load.wait()

    def gate(i, _):
        at = pl.ds(pl.multiple_of(i * 16, 16), 16)
        s = silu(gates[at, :].astype(F32))
        mixed[at, :] = mixed[at, :] * s
        grow[at, :] = grow[at, :] * s
        return 0

    lax.fori_loop(0, rows // 16, gate, 0)
    for load in w_loads:
        load.wait()
    for k in range(4):
        w_copy(k).wait_recv()

    def await_s(i, _):
        b = lax.rem(me + i, n_seq)
        s_copy(b, b).wait_recv()
        return 0

    lax.fori_loop(1, n_seq, await_s, 0)

    def y_copy(p):
        return pltpu.make_async_remote_copy(
            src_ref=y.at[p],
            dst_ref=y_mate.at[p],
            send_sem=y_s.at[p],
            recv_sem=y_r.at[p],
            device_id={"tp": mate},
            device_id_type=MESH,
        )

    def finish_rows(p):
        at = slice(p * quarter, (p + 1) * quarter)
        qm = qs[at, :]
        total = jnp.zeros((quarter, LANES), F32)
        for j in range(width // 256):
            pair = [
                s_in[(2 * j + i) * split : (2 * j + i + 1) * split].reshape(128, LANES)
                for i in range(2)
            ]
            t = dot(qm, jnp.concatenate(pair, axis=1))
            sl = slice(j * 256, (j + 1) * 256)
            x = mixed[at, sl] + grow[at, sl] * t
            mixed[at, sl] = x
            total = total + x[:, :LANES] * x[:, :LANES] + x[:, LANES:] * x[:, LANES:]
        scale = lax.rsqrt(jnp.sum(total, axis=1, keepdims=True) * (1.0 / width) + EPS)
        for j in range(slabs):
            sl = slice(j * LANES, (j + 1) * LANES)
            y[p, :, sl] = (mixed[at, sl] * scale * gain_ref[:, sl]).astype(BF16)

    def x_copy(send, recv, ss, rs, m, way):
        return pltpu.make_async_remote_copy(
            src_ref=send.at[m, way],
            dst_ref=recv.at[m, way],
            send_sem=ss.at[m, way],
            recv_sem=rs.at[m, way],
            device_id={"tp": ahead if way == 0 else behind},
            device_id_type=MESH,
        )

    def h_copy(m, way):
        return x_copy(h_send, h_recv, h_s, h_r, m, way)

    def d_copy(m, way):
        return x_copy(d_send, d_recv, d_s, d_r, m, way)

    def c_copy(m, way):
        return x_copy(c_send, c_recv, c_s, c_r, m, way)

    def chip_sum(m, k):
        rows_own = y[2 * m : 2 * m + 2].reshape(half, width)
        rows_mate = y_mate[2 * m : 2 * m + 2].reshape(half, width)
        return dot(rows_own, w_own[k]) + dot(rows_mate, w_mate[k])

    for p in range(4):
        finish_rows(p)
        if p < 2:
            y_copy(p).start()
    for p in range(4):
        first[p] = dot(y[p], w_own[0])
    for p in range(4):
        if p == 0:
            y_copy(0).wait_send()
            y_copy(1).wait_send()
            y_copy(2).start()
            y_copy(3).start()
        y_copy(p).wait_recv()
        h_send[p // 2, p % 2] = (first[p] + dot(y_mate[p], w_mate[0])).astype(BF16)
        h_copy(p // 2, p % 2).start()
    for m in range(2):
        for way in range(2):
            total = chip_sum(m, 1 + way)
            parts = total[:quarter], total[quarter:]
            d_send[m, way] = parts[1 - way].astype(BF16)
            d_copy(m, way).start()
            join[m, way] = parts[way]
    for m in range(2):
        own[m] = chip_sum(m, 3)
    for m in range(2):
        for way in range(2):
            h_copy(m, way).wait_recv()
            c_send[m, way] = (join[m, way] + h_recv[m, way].astype(F32)).astype(BF16)
            c_copy(m, way).start()
    for m in range(2):
        for way in range(2):
            d_copy(m, 1 - way).wait_recv()
            c_copy(m, way).wait_recv()
            lo = way * quarter
            total = own[m, lo : lo + quarter, :]
            total = total + d_recv[m, 1 - way].astype(F32) + c_recv[m, way].astype(F32)
            out_ref[m * half + lo : m * half + lo + quarter, :] = total.astype(BF16)

    for halo in halos:
        halo.wait_send()

    def drain(i, _):
        b = lax.rem(me + i, n_seq)
        f_copy(b, me).wait_send()
        s_copy(b, me).wait_send()
        return 0

    lax.fori_loop(1, n_seq, drain, 0)
    for i in range(1, ROW):
        a_copy(i).wait_send()
    for i in range(1, n_seq // ROW):
        b_copy(i).wait_send()
    for k in range(4):
        w_copy(k).wait_send()
    for p in range(2, 4):
        y_copy(p).wait_send()
    for m in range(2):
        for way in range(2):
            h_copy(m, way).wait_send()
            d_copy(m, way).wait_send()
            c_copy(m, way).wait_send()


def shards(
    n_seq,
    values_in,
    gates_in,
    keys_in,
    queries_in,
    log_decay,
    conv_values,
    bias_values,
    conv_keys,
    bias_keys,
    conv_queries,
    bias_queries,
    skip_scale,
    norm_gain,
    out_weight,
):
    rows, width = values_in.shape
    heads = log_decay.shape[0]
    chunks = rows // CH
    slabs = width // LANES
    seg = 128 * slabs // n_seq
    half, quarter = rows // 2, rows // 4
    depth, full = out_weight.shape
    cols = full // 8
    hbm = pl.BlockSpec(memory_space=pl.ANY)
    dma = pltpu.SemaphoreType.DMA
    args = (
        values_in,
        gates_in,
        keys_in,
        queries_in,
        log_decay,
        conv_values,
        bias_values[None],
        conv_keys,
        bias_keys[None],
        conv_queries,
        bias_queries[None],
        skip_scale[None],
        norm_gain[None],
        out_weight,
    )
    return pl.pallas_call(
        functools.partial(kernel, n_seq),
        out_shape=jax.ShapeDtypeStruct((rows, cols), BF16),
        in_specs=[hbm] * len(args),
        out_specs=pl.BlockSpec(memory_space=pltpu.VMEM),
        scratch_shapes=[pltpu.VMEM(a.shape, a.dtype) for a in args[4:13]]
        + [
            pltpu.VMEM((rows + PAD, width + 256), BF16),
            pltpu.VMEM((PAD, width + 256), BF16),
            pltpu.VMEM((rows, width), BF16),
            pltpu.VMEM((4, depth, cols), BF16),
            pltpu.VMEM((4, depth, cols), BF16),
            pltpu.VMEM((2 * heads, width), BF16),
            pltpu.VMEM((3 * PAD, 2 * PAD), BF16),
            pltpu.VMEM((chunks, CH, heads), F32),
            pltpu.VMEM((chunks, heads, CH), F32),
            pltpu.VMEM((rows, width), F32),
            pltpu.VMEM((rows, width), F32),
            pltpu.VMEM((chunks, 8, width), F32),
            pltpu.VMEM((chunks, 8, width), F32),
            pltpu.VMEM((rows, width), BF16),
            pltpu.VMEM((CH, width), BF16),
            pltpu.VMEM((CH, 128), BF16),
            pltpu.VMEM((chunks, 128, CH), BF16),
            pltpu.VMEM((rows, 128), BF16),
            pltpu.VMEM((chunks, 128, width), F32),
            pltpu.VMEM((128, width), F32),
            pltpu.VMEM((chunks, 128, width), BF16),
            pltpu.VMEM((rows, width), F32),
            pltpu.VMEM((slabs, LANES), F32),
            pltpu.VMEM((n_seq, slabs, LANES), F32),
            pltpu.VMEM((n_seq, seg, LANES), BF16),
            pltpu.VMEM((n_seq, seg, LANES), BF16),
            pltpu.VMEM((n_seq, seg, LANES), BF16),
            pltpu.VMEM((n_seq, seg, LANES), BF16),
            pltpu.VMEM((4, quarter, width), BF16),
            pltpu.VMEM((4, quarter, width), BF16),
            pltpu.VMEM((4, quarter, cols), F32),
            pltpu.VMEM((2, half, cols), F32),
            pltpu.VMEM((2, 2, quarter, cols), F32),
        ]
        + [pltpu.VMEM((2, 2, quarter, cols), BF16)] * 6
        + [dma((9,)), dma((4,)), dma((4,)), dma((4,)), dma((4,)), dma((3,)), dma((3,))]
        + [dma((ROW,))] * 2
        + [dma((n_seq // ROW,))] * 2
        + [dma((n_seq,))] * 4
        + [dma((4,))] * 2
        + [dma((2, 2))] * 6,
        compiler_params=pltpu.CompilerParams(
            collective_id=0, has_side_effects=True, vmem_limit_bytes=48 * 2**20
        ),
        name="mixer",
    )(*[pltpu.with_memory_space_constraint(a, pltpu.HBM) for a in args])


def solution(mesh):
    placed = (
        P("seq", "tp"),
        P("seq", "tp"),
        P("seq", "tp"),
        P("seq", "tp"),
        P("tp", "seq"),
        P(None, "tp"),
        P("tp"),
        P(None, "tp"),
        P("tp"),
        P(None, "tp"),
        P("tp"),
        P("tp"),
        P("tp"),
        P("tp", None),
    )
    return jax.shard_map(
        functools.partial(shards, mesh.shape["seq"]),
        mesh=mesh,
        in_specs=placed,
        out_specs=P("seq", "tp"),
        check_vma=False,
    )
```

```python
import functools

import jax
import jax.numpy as jnp
from jax import lax
from jax.experimental import pallas as pl
from jax.experimental.pallas import tpu as pltpu
from jax.sharding import PartitionSpec as P

MESH = pl.DeviceIdType.MESH
F32 = jnp.float32
BF16 = jnp.bfloat16
EPS = 1e-05
CH = 128
PAD = 16
LANES = 128
ROW = 8
EARLY = 9


def dot(a, b):
    return jnp.dot(a, b, preferred_element_type=F32)


def silu(v):
    h = 0.5 * v
    return h + h * jnp.tanh(h)


def parts_of(x):
    hi = x.astype(BF16).astype(F32)
    rest = x - hi
    mid = rest.astype(BF16).astype(F32)
    return hi, mid, rest - mid


def kernel(
    n_seq,
    v_hbm,
    g_hbm,
    k_hbm,
    q_hbm,
    log_hbm,
    cv_hbm,
    bv_hbm,
    ck_hbm,
    bk_hbm,
    cq_hbm,
    bq_hbm,
    skip_hbm,
    gain_hbm,
    w_hbm,
    out_ref,
    log_ref,
    cv_ref,
    bv_ref,
    ck_ref,
    bk_ref,
    cq_ref,
    bq_ref,
    skip_ref,
    gain_ref,
    xpad,
    edge,
    gates,
    w_own,
    w_mate,
    spread,
    shift_top,
    ct,
    cs,
    grow,
    rem,
    dec,
    ap,
    vals,
    vw,
    keys0,
    keys_t,
    qs,
    fresh,
    rest,
    s_loc,
    mixed,
    abuf,
    ra,
    fbuf,
    rf,
    sbuf,
    s_in,
    y,
    y_mate,
    first,
    own,
    join,
    h_send,
    h_recv,
    d_send,
    d_recv,
    c_send,
    c_recv,
    small_sem,
    in_sem,
    w_sem,
    wx_s,
    wx_r,
    halo_s,
    halo_r,
    a_s,
    a_r,
    b_s,
    b_r,
    f_s,
    f_r,
    s_s,
    s_r,
    y_s,
    y_r,
    h_s,
    h_r,
    d_s,
    d_r,
    c_s,
    c_r,
):
    rows, width = v_hbm.shape
    heads = log_ref.shape[0]
    hops = sorted(
        ((dy, dz) for dy in range(n_seq // ROW) for dz in range(ROW) if dy or dz),
        key=lambda o: -min(o[0], n_seq // ROW - o[0]) - min(o[1], ROW - o[1]),
    )
    chunks = rows // CH
    slabs = width // LANES
    split = n_seq // slabs
    seg = 128 // split
    half = rows // 2
    quarter = half // 2
    tp_size = lax.axis_size("tp")
    me = lax.axis_index("seq")
    tp = lax.axis_index("tp")
    core = lax.rem(tp, 2)
    mate = tp + 1 - 2 * core
    ahead = lax.rem(tp + 2, tp_size)
    behind = lax.rem(tp + tp_size - 2, tp_size)
    far = lax.rem(tp + 4, tp_size)

    barrier = pltpu.get_barrier_semaphore()

    def greet(i, _):
        pl.semaphore_signal(
            barrier, inc=1, device_id={"seq": lax.rem(me + i, n_seq)}, device_id_type=MESH
        )
        return 0

    lax.fori_loop(1, n_seq, greet, 0)
    for other in (mate, ahead, behind):
        pl.semaphore_signal(barrier, inc=1, device_id={"tp": other}, device_id_type=MESH)

    smalls = [
        pltpu.make_async_copy(src, dst, small_sem.at[i])
        for i, (src, dst) in enumerate(
            (
                (log_hbm, log_ref),
                (cv_hbm, cv_ref),
                (bv_hbm, bv_ref),
                (ck_hbm, ck_ref),
                (bk_hbm, bk_ref),
                (cq_hbm, cq_ref),
                (bq_hbm, bq_ref),
                (skip_hbm, skip_ref),
                (gain_hbm, gain_ref),
            )
        )
    ]
    loads = [
        pltpu.make_async_copy(v_hbm, xpad.at[pl.ds(PAD, rows), pl.ds(0, width)], in_sem.at[0]),
        pltpu.make_async_copy(
            k_hbm, xpad.at[pl.ds(PAD, rows), pl.ds(width, 128)], in_sem.at[1]
        ),
        pltpu.make_async_copy(
            q_hbm, xpad.at[pl.ds(PAD, rows), pl.ds(width + 128, 128)], in_sem.at[2]
        ),
    ]
    gate_load = pltpu.make_async_copy(g_hbm, gates, in_sem.at[3])
    for load in smalls + loads:
        load.start()
    cols = w_hbm.shape[1] // tp_size

    def w_part(k, side):
        chip = (far, ahead, behind, tp)[k] - core
        return w_hbm.at[:, pl.ds(pl.multiple_of((chip + side) * cols, cols), cols)]

    w_loads = [
        pltpu.make_async_copy(w_part(k, core), w_own.at[k], w_sem.at[k]) for k in range(4)
    ]

    def w_copy(k):
        return pltpu.make_async_remote_copy(
            src_ref=w_part(k, 1 - core),
            dst_ref=w_mate.at[k],
            send_sem=wx_s.at[k],
            recv_sem=wx_r.at[k],
            device_id={"tp": mate},
            device_id_type=MESH,
        )

    xpad[0:PAD, :] = jnp.zeros((PAD, xpad.shape[1]), BF16)
    for ref, span in ((shift_top, PAD),):
        out_row = lax.broadcasted_iota(jnp.int32, ref.shape, 0)
        in_row = lax.broadcasted_iota(jnp.int32, ref.shape, 1)
        hit = out_row == -1
        for back in range(1, 4):
            base = (back - 1) * span
            here = (out_row >= base) & (out_row < base + span)
            hit = hit | (here & (in_row == out_row - base + PAD - back))
        ref[...] = jnp.where(hit, 1.0, 0.0).astype(BF16)

    lane_head = lax.broadcasted_iota(jnp.int32, (2 * heads, width), 1) // (width // heads)
    row_head = lax.broadcasted_iota(jnp.int32, (2 * heads, width), 0)
    row_head = jnp.where(row_head >= heads, row_head - heads, row_head)
    spread[...] = jnp.where(lane_head == row_head, 1.0, 0.0).astype(BF16)

    def expand(x):
        hi = x.astype(BF16).astype(F32)
        return jnp.concatenate([hi, x - hi], axis=1).astype(BF16)

    low_a = lax.broadcasted_iota(jnp.int32, (CH, CH), 0)
    low_b = lax.broadcasted_iota(jnp.int32, (CH, CH), 1)
    lower = jnp.where(low_b <= low_a, 1.0, 0.0)
    lower3 = jnp.concatenate([lower] * 3, axis=1).astype(BF16)
    upper = jnp.where(low_a <= low_b, 1.0, 0.0)
    upper3 = jnp.concatenate([upper] * 3, axis=0).astype(BF16)

    def decay(c, _):
        at = pl.ds(pl.multiple_of(c * CH, CH), CH)
        logs = jnp.concatenate(parts_of(log_ref[:, at]), axis=1).astype(BF16)
        col = lax.dot_general(lower3, logs, (((1,), (1,)), ((), ())), preferred_element_type=F32)
        ct[c] = col
        cs[c] = dot(logs, upper3)
        last = expand(jnp.exp(col[CH - 8 :, :]))
        r2 = expand(jnp.exp(jnp.minimum(col[CH - 1 : CH, :] - col, 0.0)))
        for j in range(width // 256):
            sl = slice(j * 256, (j + 1) * 256)
            dec[c, :, sl] = dot(last, spread[:, sl])
            rem[at, sl] = dot(r2, spread[:, sl])
        return 0

    smalls[0].wait()
    lax.fori_loop(0, chunks, decay, 0)
    before = jnp.ones((1, width), F32)
    for c in range(chunks):
        ap[c] = jnp.broadcast_to(before, (8, width))
        before = before * dec[c, 7:8, :]
    for q in range(slabs):
        abuf[q : q + 1, :] = before[:, q * LANES : (q + 1) * LANES]
    after = {"seq": lax.rem(me + 1, n_seq)}
    halos = []
    for i, (src, lo, wid) in enumerate(
        ((v_hbm, 0, width), (k_hbm, width, 128), (q_hbm, width + 128, 128))
    ):
        halos.append(
            pltpu.make_async_remote_copy(
                src_ref=src.at[pl.ds(rows - PAD, PAD), :],
                dst_ref=edge.at[:, pl.ds(lo, wid)],
                send_sem=halo_s.at[i],
                recv_sem=halo_r.at[i],
                device_id=after,
                device_id_type=MESH,
            )
        )

    row, col = me // ROW, lax.rem(me, ROW)

    def a_copy(i):
        return pltpu.make_async_remote_copy(
            src_ref=abuf,
            dst_ref=ra.at[me],
            send_sem=a_s.at[i],
            recv_sem=a_r.at[i],
            device_id={"seq": row * ROW + lax.rem(col + i, ROW)},
            device_id_type=MESH,
        )

    def b_copy(i):
        mine = pl.ds(pl.multiple_of(row * ROW, ROW), ROW)
        return pltpu.make_async_remote_copy(
            src_ref=ra.at[mine],
            dst_ref=ra.at[mine],
            send_sem=b_s.at[i],
            recv_sem=b_r.at[i],
            device_id={"seq": lax.rem(row + i, n_seq // ROW) * ROW + col},
            device_id_type=MESH,
        )

    def f_copy(peer, slot):
        return pltpu.make_async_remote_copy(
            src_ref=fbuf.at[peer],
            dst_ref=rf.at[slot],
            send_sem=f_s.at[peer],
            recv_sem=f_r.at[slot],
            device_id={"seq": peer},
            device_id_type=MESH,
        )

    def s_copy(peer, slot):
        return pltpu.make_async_remote_copy(
            src_ref=sbuf.at[peer],
            dst_ref=s_in.at[slot],
            send_sem=s_s.at[peer],
            recv_sem=s_r.at[slot],
            device_id={"seq": peer},
            device_id_type=MESH,
        )

    def taps(x, shifted, span, w_ref, b_ref, sl):
        acc = b_ref[:, sl] + w_ref[3:4, sl] * x.astype(F32)
        for back in range(1, 4):
            acc = acc + w_ref[3 - back : 4 - back, sl] * shifted[(back - 1) * span : back * span]
        return silu(acc).astype(BF16)

    def rolled(window, lo, w_ref, b_ref, sl):
        x = xpad[window, lo : lo + LANES].astype(F32)
        w = 0.5 * w_ref[:, sl]
        acc = 0.5 * b_ref[:, sl] + w[3:4] * x[PAD:]
        for back in range(1, 4):
            acc = acc + w[3 - back : 4 - back] * pltpu.roll(x, back, axis=0)[PAD:]
        return (acc + acc * jnp.tanh(acc)).astype(BF16)

    def conv(c, top):
        at = pl.ds(pl.multiple_of(c * CH, CH), CH)
        window = pl.ds(pl.multiple_of(c * CH, CH), CH + PAD)
        one = slice(0, 128)
        keys = rolled(window, width, ck_ref, bk_ref, one)
        kt = keys.astype(F32).T.astype(BF16)
        keys_t[c] = kt
        if top:
            keys0[...] = keys
        for j in range(slabs):
            sl = slice(j * LANES, (j + 1) * LANES)
            v = rolled(window, j * LANES, cv_ref, bv_ref, sl)
            vals[at, sl] = v
            vw[:, sl] = (v.astype(F32) * rem[at, sl]).astype(BF16)
            if top:
                vw[0:PAD, sl] = jnp.zeros((PAD, LANES), BF16)
        for j in range(width // 256):
            sl = slice(j * 256, (j + 1) * 256)
            fresh[c, :, sl] = dot(kt, vw[:, sl])

    for load in smalls[1:] + loads:
        load.wait()
    gate_load.start()
    for load in w_loads:
        load.start()

    def conv_step(i, _):
        conv(chunks - i, False)
        return 0


    pl.semaphore_wait(barrier, n_seq - 1 + 3)
    for halo in halos:
        halo.start()
    for i in range(1, ROW):
        a_copy(i).start()
    ra[me] = abuf[...]
    lax.fori_loop(1, chunks, conv_step, 0)
    conv(0, True)
    for q in range(slabs):
        sl = slice(q * LANES, (q + 1) * LANES)
        s = fresh[0, :, sl]
        for c in range(1, chunks):
            s = dec[c, 7:8, sl] * s + fresh[c, :, sl]
        rest[:, sl] = s

    later = jnp.ones((1, width), F32)
    for c in range(1, chunks):
        later = later * dec[c, 7:8, :]
    is_first = me == 0
    for halo in halos:
        halo.wait_recv()
    head = slice(0, PAD)

    def top_rows(sl):
        above = jnp.where(is_first, 0.0, edge[:, sl].astype(F32)).astype(BF16)
        here = xpad[PAD : 2 * PAD, sl]
        return here, dot(shift_top[...], jnp.concatenate([above, here], axis=0))

    x_top, moved_top = top_rows(slice(width, width + 256))
    keys0[head, :] = taps(
        x_top[:, :128], moved_top[:, :128], PAD, ck_ref, bk_ref, slice(0, 128)
    )
    kt = keys0[...].astype(F32).T.astype(BF16)
    keys_t[0] = kt
    for j in range(width // 256):
        sl = slice(j * 256, (j + 1) * 256)
        x, moved = top_rows(sl)
        v = taps(x, moved, PAD, cv_ref, bv_ref, sl)
        vals[head, sl] = v
        weighted = (v.astype(F32) * rem[head, sl]).astype(BF16)
        more = dot(kt[:, :PAD], weighted)
        fresh[0, :, sl] = fresh[0, :, sl] + more
        f = (rest[:, sl] + later[:, sl] * more).astype(BF16)
        for i in range(2):
            for r in range(split):
                fbuf[(2 * j + i) * split + r] = f[
                    r * seg : (r + 1) * seg, i * LANES : (i + 1) * LANES
                ]

    def far_first(copy):
        for dy, dz in hops:
            at = lax.rem(me // ROW + dy, n_seq // ROW) * ROW + lax.rem(lax.rem(me, ROW) + dz, ROW)
            copy(at, me).start()

    far_first(f_copy)
    rf[me] = fbuf[me]
    for k in range(4):
        w_copy(k).start()

    def query(c, _):
        at = pl.ds(pl.multiple_of(c * CH, CH), CH)
        window = pl.ds(pl.multiple_of(c * CH, CH), CH + PAD)
        qs[at, :] = rolled(window, width + 128, cq_ref, bq_ref, slice(0, 128))
        return 0

    lax.fori_loop(0, chunks, query, 0)
    qs[head, :] = taps(
        x_top[:, 128:], moved_top[:, 128:], PAD, cq_ref, bq_ref, slice(0, 128)
    )
    for i in range(1, ROW):
        a_copy(i).wait_recv()
    for i in range(1, n_seq // ROW):
        b_copy(i).start()

    for q in range(slabs):
        sl = slice(q * LANES, (q + 1) * LANES)
        s = fresh[0, :, sl]
        s_loc[0, :, sl] = jnp.zeros((128, LANES), BF16)
        for c in range(1, chunks):
            s_loc[c, :, sl] = s.astype(BF16)
            s = dec[c, 7:8, sl] * s + fresh[c, :, sl]

    skip8 = jnp.broadcast_to(skip_ref[...], (8, heads))
    skip_row = dot(expand(skip8), spread[...])
    lane = lax.broadcasted_iota(jnp.int32, (1, LANES), 1)
    front = jnp.where(lane < LANES // 2, 1.0, 0.0).astype(BF16)
    back_half = jnp.where(lane < LANES // 2, 0.0, 1.0).astype(BF16)

    def local(c, _):
        at = pl.ds(pl.multiple_of(c * CH, CH), CH)
        qc = qs[at, :]
        g2 = expand(jnp.exp(ct[c]))
        scores = jnp.where(low_b <= low_a, dot(qc, keys_t[c]), 0.0)
        for q in range(slabs):
            sl = slice(q * LANES, (q + 1) * LANES)
            mixes = []
            for h in (2 * q, 2 * q + 1):
                gap = ct[c, :, h : h + 1] - cs[c, h : h + 1, :]
                mixes.append((jnp.exp(jnp.minimum(gap, 0.0)) * scores).astype(BF16))
            v = vals[at, sl]
            rhs = jnp.concatenate([v * front, v * back_half], axis=0)
            o = dot(jnp.concatenate(mixes, axis=1), rhs)
            g = dot(g2, spread[:, sl])
            o = o + g * dot(qc, s_loc[c, :, sl])
            mixed[at, sl] = o + skip_row[0:1, sl] * v.astype(F32)
            grow[at, sl] = g * ap[c, 0:1, sl]
        return 0

    lax.fori_loop(0, chunks, local, 0)

    for i in range(1, n_seq // ROW):
        b_copy(i).wait_recv()
    state = jnp.zeros((seg // 8, 8, LANES), F32)
    for b in range(n_seq):
        @pl.when(me != b)
        def _(b=b):
            f_copy(b, b).wait_recv()

        sbuf[b] = state.astype(BF16).reshape(seg, LANES)
        if b < EARLY:

            @pl.when(me != b)
            def _(b=b):
                s_copy(b, me).start()

        state = ra[b, pl.ds(me // split, 1), :][None] * state + rf[b].astype(F32).reshape(seg // 8, 8, LANES)
    for dy, dz in hops:
        at = lax.rem(row + dy, n_seq // ROW) * ROW + lax.rem(col + dz, ROW)

        @pl.when(at >= EARLY)
        def _(at=at):
            s_copy(at, me).start()

    s_in[me] = sbuf[me]

    gate_load.wait()

    def gate(i, _):
        at = pl.ds(pl.multiple_of(i * 16, 16), 16)
        s = silu(gates[at, :].astype(F32))
        mixed[at, :] = mixed[at, :] * s
        grow[at, :] = grow[at, :] * s
        return 0

    lax.fori_loop(0, rows // 16, gate, 0)
    for load in w_loads:
        load.wait()
    for k in range(4):
        w_copy(k).wait_recv()

    def await_s(i, _):
        b = lax.rem(me + i, n_seq)
        s_copy(b, b).wait_recv()
        return 0

    lax.fori_loop(1, n_seq, await_s, 0)

    def y_copy(p):
        return pltpu.make_async_remote_copy(
            src_ref=y.at[p],
            dst_ref=y_mate.at[p],
            send_sem=y_s.at[p],
            recv_sem=y_r.at[p],
            device_id={"tp": mate},
            device_id_type=MESH,
        )

    def finish_rows(p):
        at = slice(p * quarter, (p + 1) * quarter)
        qm = qs[at, :]
        total = jnp.zeros((quarter, LANES), F32)
        for j in range(width // 256):
            pair = [
                s_in[(2 * j + i) * split : (2 * j + i + 1) * split].reshape(128, LANES)
                for i in range(2)
            ]
            t = dot(qm, jnp.concatenate(pair, axis=1))
            sl = slice(j * 256, (j + 1) * 256)
            x = mixed[at, sl] + grow[at, sl] * t
            mixed[at, sl] = x
            total = total + x[:, :LANES] * x[:, :LANES] + x[:, LANES:] * x[:, LANES:]
        scale = lax.rsqrt(jnp.sum(total, axis=1, keepdims=True) * (1.0 / width) + EPS)
        for j in range(slabs):
            sl = slice(j * LANES, (j + 1) * LANES)
            y[p, :, sl] = (mixed[at, sl] * scale * gain_ref[:, sl]).astype(BF16)

    def x_copy(send, recv, ss, rs, m, way):
        return pltpu.make_async_remote_copy(
            src_ref=send.at[m, way],
            dst_ref=recv.at[m, way],
            send_sem=ss.at[m, way],
            recv_sem=rs.at[m, way],
            device_id={"tp": ahead if way == 0 else behind},
            device_id_type=MESH,
        )

    def h_copy(m, way):
        return x_copy(h_send, h_recv, h_s, h_r, m, way)

    def d_copy(m, way):
        return x_copy(d_send, d_recv, d_s, d_r, m, way)

    def c_copy(m, way):
        return x_copy(c_send, c_recv, c_s, c_r, m, way)

    def chip_sum(m, k):
        rows_own = y[2 * m : 2 * m + 2].reshape(half, width)
        rows_mate = y_mate[2 * m : 2 * m + 2].reshape(half, width)
        return dot(rows_own, w_own[k]) + dot(rows_mate, w_mate[k])

    for p in range(4):
        finish_rows(p)
        if p < 2:
            y_copy(p).start()
    for p in range(4):
        first[p] = dot(y[p], w_own[0])
    for p in range(4):
        if p == 0:
            y_copy(0).wait_send()
            y_copy(1).wait_send()
            y_copy(2).start()
            y_copy(3).start()
        y_copy(p).wait_recv()
        h_send[p // 2, p % 2] = (first[p] + dot(y_mate[p], w_mate[0])).astype(BF16)
        h_copy(p // 2, p % 2).start()
    for m in range(2):
        for way in range(2):
            total = chip_sum(m, 1 + way)
            parts = total[:quarter], total[quarter:]
            d_send[m, way] = parts[1 - way].astype(BF16)
            d_copy(m, way).start()
            join[m, way] = parts[way]
    for m in range(2):
        own[m] = chip_sum(m, 3)
    for m in range(2):
        for way in range(2):
            h_copy(m, way).wait_recv()
            c_send[m, way] = (join[m, way] + h_recv[m, way].astype(F32)).astype(BF16)
            c_copy(m, way).start()
    for halo in halos:
        halo.wait_send()

    def drain(i, _):
        b = lax.rem(me + i, n_seq)
        f_copy(b, me).wait_send()
        s_copy(b, me).wait_send()
        return 0

    lax.fori_loop(1, n_seq, drain, 0)
    for i in range(1, ROW):
        a_copy(i).wait_send()
    for i in range(1, n_seq // ROW):
        b_copy(i).wait_send()
    for k in range(4):
        w_copy(k).wait_send()
    for p in range(2, 4):
        y_copy(p).wait_send()
    for m in range(2):
        for way in range(2):
            d_copy(m, 1 - way).wait_recv()
            c_copy(m, way).wait_recv()
            lo = way * quarter
            total = own[m, lo : lo + quarter, :]
            total = total + d_recv[m, 1 - way].astype(F32) + c_recv[m, way].astype(F32)
            out_ref[m * half + lo : m * half + lo + quarter, :] = total.astype(BF16)

    for m in range(2):
        for way in range(2):
            h_copy(m, way).wait_send()
            d_copy(m, way).wait_send()
            c_copy(m, way).wait_send()


def shards(
    n_seq,
    values_in,
    gates_in,
    keys_in,
    queries_in,
    log_decay,
    conv_values,
    bias_values,
    conv_keys,
    bias_keys,
    conv_queries,
    bias_queries,
    skip_scale,
    norm_gain,
    out_weight,
):
    rows, width = values_in.shape
    heads = log_decay.shape[0]
    chunks = rows // CH
    slabs = width // LANES
    seg = 128 * slabs // n_seq
    half, quarter = rows // 2, rows // 4
    depth, full = out_weight.shape
    cols = full // 8
    hbm = pl.BlockSpec(memory_space=pl.ANY)
    dma = pltpu.SemaphoreType.DMA
    args = (
        values_in,
        gates_in,
        keys_in,
        queries_in,
        log_decay,
        conv_values,
        bias_values[None],
        conv_keys,
        bias_keys[None],
        conv_queries,
        bias_queries[None],
        skip_scale[None],
        norm_gain[None],
        out_weight,
    )
    return pl.pallas_call(
        functools.partial(kernel, n_seq),
        out_shape=jax.ShapeDtypeStruct((rows, cols), BF16),
        in_specs=[hbm] * len(args),
        out_specs=pl.BlockSpec(memory_space=pltpu.VMEM),
        scratch_shapes=[pltpu.VMEM(a.shape, a.dtype) for a in args[4:13]]
        + [
            pltpu.VMEM((rows + PAD, width + 256), BF16),
            pltpu.VMEM((PAD, width + 256), BF16),
            pltpu.VMEM((rows, width), BF16),
            pltpu.VMEM((4, depth, cols), BF16),
            pltpu.VMEM((4, depth, cols), BF16),
            pltpu.VMEM((2 * heads, width), BF16),
            pltpu.VMEM((3 * PAD, 2 * PAD), BF16),
            pltpu.VMEM((chunks, CH, heads), F32),
            pltpu.VMEM((chunks, heads, CH), F32),
            pltpu.VMEM((rows, width), F32),
            pltpu.VMEM((rows, width), F32),
            pltpu.VMEM((chunks, 8, width), F32),
            pltpu.VMEM((chunks, 8, width), F32),
            pltpu.VMEM((rows, width), BF16),
            pltpu.VMEM((CH, width), BF16),
            pltpu.VMEM((CH, 128), BF16),
            pltpu.VMEM((chunks, 128, CH), BF16),
            pltpu.VMEM((rows, 128), BF16),
            pltpu.VMEM((chunks, 128, width), F32),
            pltpu.VMEM((128, width), F32),
            pltpu.VMEM((chunks, 128, width), BF16),
            pltpu.VMEM((rows, width), F32),
            pltpu.VMEM((slabs, LANES), F32),
            pltpu.VMEM((n_seq, slabs, LANES), F32),
            pltpu.VMEM((n_seq, seg, LANES), BF16),
            pltpu.VMEM((n_seq, seg, LANES), BF16),
            pltpu.VMEM((n_seq, seg, LANES), BF16),
            pltpu.VMEM((n_seq, seg, LANES), BF16),
            pltpu.VMEM((4, quarter, width), BF16),
            pltpu.VMEM((4, quarter, width), BF16),
            pltpu.VMEM((4, quarter, cols), F32),
            pltpu.VMEM((2, half, cols), F32),
            pltpu.VMEM((2, 2, quarter, cols), F32),
        ]
        + [pltpu.VMEM((2, 2, quarter, cols), BF16)] * 6
        + [dma((9,)), dma((4,)), dma((4,)), dma((4,)), dma((4,)), dma((3,)), dma((3,))]
        + [dma((ROW,))] * 2
        + [dma((n_seq // ROW,))] * 2
        + [dma((n_seq,))] * 4
        + [dma((4,))] * 2
        + [dma((2, 2))] * 6,
        compiler_params=pltpu.CompilerParams(
            collective_id=0, has_side_effects=True, vmem_limit_bytes=48 * 2**20
        ),
        name="mixer",
    )(*[pltpu.with_memory_space_constraint(a, pltpu.HBM) for a in args])


def solution(mesh):
    placed = (
        P("seq", "tp"),
        P("seq", "tp"),
        P("seq", "tp"),
        P("seq", "tp"),
        P("tp", "seq"),
        P(None, "tp"),
        P("tp"),
        P(None, "tp"),
        P("tp"),
        P(None, "tp"),
        P("tp"),
        P("tp"),
        P("tp"),
        P("tp", None),
    )
    return jax.shard_map(
        functools.partial(shards, mesh.shape["seq"]),
        mesh=mesh,
        in_specs=placed,
        out_specs=P("seq", "tp"),
        check_vma=False,
    )
```
